32 devices in a mesh: vel: 4 (over y, x), cell: 8 (over z, core).
Axes of the slice: x: 2, y: 2, z: 4, core: 2. Of those that a mesh axis runs over, the one named last changes fastest.
Arguments:
- distribution: float32 [32, 32, 13824], P('cell', None, 'vel'), may hold values from -6 to 6
- collision: bfloat16 [4, 8, 432, 13824], P(None, 'cell', None, 'vel'), may hold values from -0.0546875 to 0.0546875
- directions: int32 [13824], P('vel'), may hold values from 0 to 1
- wall_mask: int32 [32, 32], P('cell'), may hold values 0 or 1
Outputs:
- relaxed: float32 [32, 32, 13824], P('cell', None, 'vel')
The draws below stay inside these ranges and needn't reach their ends.
All inputs are finite; a program needn't handle non-finite values. No bound on the sum of `wall_mask` on one device may be relied on, other than what follows from the above.
Results may differ from the reference program's by a relative error of at most 0.0012.
Values may be sent and summed in bfloat16 or wider, within the bound.
No kernel may reach another device: no remote copies, remote signals or barrier semaphores. Data moves between devices by JAX's collectives and lax.ppermute only.
A program may use at most 128 MiB of HBM per device.

```python
import jax
import jax.numpy as jnp
from jax import lax

VG = 24
VELOCITY_COUNT = 13824
PIECE_VELOCITIES = 432
CHANNEL_WIDTH = 32
CHANNEL_LENGTH = 32
N_VEL = 4
N_CELL = 8


def touch_ends(drawn, own_key, smallest, largest):
    extent = drawn.shape
    place = [jax.random.randint(jax.random.fold_in(own_key, axis), (), 0, extent[axis]) for axis in range(len(extent))]
    drawn = drawn.at[tuple(place)].set(smallest)
    longest = extent.index(max(extent))
    place[longest] = (place[longest] + 1) % extent[longest]
    return drawn.at[tuple(place)].set(largest)


def levels(stream_key, shape, pieces, low, high):
    def one(dim, shards_of):
        steps = jax.random.uniform(jax.random.fold_in(jax.random.fold_in(stream_key, 6), dim), (shards_of,), jnp.float32, low / len(pieces), high / len(pieces))
        return jnp.repeat(jnp.exp(steps), shape[dim] // shards_of).reshape((-1,) + (1,) * (len(shape) - dim - 1))

    level = one(*pieces[0])
    for cut in pieces[1:]:
        level = level * one(*cut)
    return level


def gaussian(stream_key, shape, deviation, reach, split=(), kind=jnp.bfloat16):
    values = jax.random.normal(stream_key, shape, jnp.float32) * deviation
    if len(split) > 0:
        values = levels(stream_key, shape, split, -0.22, 0.18) * values
    return jnp.clip(values, min=-reach, max=reach).astype(kind)


def setup_inputs(seed: int = 0) -> dict:
    arg_keys = jax.random.split(jax.random.key(seed), 5)
    return {
        "distribution": gaussian(arg_keys[0], (CHANNEL_LENGTH, CHANNEL_WIDTH, VELOCITY_COUNT), 1.0, 6.0, ((0, 8), (2, 4)), jnp.float32),
        "collision": gaussian(arg_keys[1], (N_VEL, N_CELL, PIECE_VELOCITIES, VELOCITY_COUNT), VELOCITY_COUNT ** -0.5, 0.0546875, ((1, 8), (3, 4))),
        "directions": touch_ends(jax.random.randint(arg_keys[2], (VELOCITY_COUNT,), 0, 2), jax.random.fold_in(arg_keys[2], 1), 0, 1).astype(jnp.int32),
        "wall_mask": touch_ends((jax.random.randint(arg_keys[3], (CHANNEL_LENGTH, CHANNEL_WIDTH), 0, 8) < 1).astype(jnp.int32), jax.random.fold_in(arg_keys[3], 1), 0, 1),
    }


courant = 0.8
relax = 0.5


def speeds(directions, offset, length):
    vel_index = offset + jnp.arange(length, dtype=jnp.int32)
    grid_x = vel_index // (VG * VG)
    grid_y = (vel_index // VG) % VG
    moving = 2 * directions - 1
    speed_x = courant * (grid_x.astype(jnp.float32) + 0.5) / VG
    speed_y = courant * (grid_y.astype(jnp.float32) - 0.5 * (VG - 1)) / VG
    return moving, speed_x, speed_y


def transverse(distribution, speed_y):
    width_y = distribution.shape[1]
    padded = jnp.pad(distribution, ((0, 0), (2, 2), (0, 0)))
    upward = speed_y > 0
    first_up = jnp.where(upward, padded[:, 1:width_y + 1], padded[:, 3:width_y + 3])
    second_up = jnp.where(upward, padded[:, 0:width_y], padded[:, 4:width_y + 4])
    return jnp.abs(speed_y) * (1.5 * distribution - 2.0 * first_up + 0.5 * second_up)


def reference(distribution, collision, directions, wall_mask):
    moving, speed_x, speed_y = speeds(directions, 0, VELOCITY_COUNT)
    first_up = jnp.where(moving > 0, jnp.roll(distribution, 1, axis=0), jnp.roll(distribution, -1, axis=0))
    second_up = jnp.where(moving > 0, jnp.roll(distribution, 2, axis=0), jnp.roll(distribution, -2, axis=0))
    adv_x = speed_x * (1.5 * distribution - 2.0 * first_up + 0.5 * second_up)
    adv_y = transverse(distribution, speed_y)
    panel_block = distribution.astype(jnp.bfloat16).reshape(CHANNEL_LENGTH * CHANNEL_WIDTH, N_VEL, N_CELL, PIECE_VELOCITIES)

    def add_group(total, velocity_group):
        column_list = lax.dynamic_index_in_dim(panel_block, velocity_group, 2, keepdims=False).reshape(CHANNEL_LENGTH * CHANNEL_WIDTH, N_VEL * PIECE_VELOCITIES)
        row_list = lax.dynamic_index_in_dim(collision, velocity_group, 1, keepdims=False).reshape(N_VEL * PIECE_VELOCITIES, VELOCITY_COUNT)
        part = jnp.dot(column_list, row_list, preferred_element_type=jnp.float32)
        return total + part, None

    start = jnp.zeros((CHANNEL_LENGTH * CHANNEL_WIDTH, VELOCITY_COUNT), jnp.float32)
    gain, _ = lax.scan(add_group, start, jnp.arange(N_CELL, dtype=jnp.int32))
    gain = gain.reshape(CHANNEL_LENGTH, CHANNEL_WIDTH, VELOCITY_COUNT)
    open_cells = (1 - wall_mask).astype(jnp.float32)[:, :, None]
    return open_cells * (distribution - adv_x - adv_y + relax * gain)
```

```python
import functools

import jax
import jax.numpy as jnp
from jax import lax
from jax.experimental import pallas as pl
from jax.experimental.pallas import tpu as pltpu
from jax.sharding import PartitionSpec as P

VG = 24
courant = 0.8
relax = 0.5
COLLISION_MAX = 0.0546875
TAIL = 16
LANES = 128
BF16 = jnp.bfloat16
F16 = jnp.float16
F32 = jnp.float32


def speeds(directions, offset, length):
    vel_index = offset + jnp.arange(length, dtype=jnp.int32)
    grid_x = vel_index // (VG * VG)
    grid_y = vel_index // VG % VG
    moving = 2 * directions - 1
    speed_x = courant * (grid_x.astype(F32) + 0.5) / VG
    speed_y = courant * (grid_y.astype(F32) - 0.5 * (VG - 1)) / VG
    return (moving, speed_x, speed_y)


def transverse(distribution, speed_y):
    width_y = distribution.shape[1]
    padded = jnp.pad(distribution, ((0, 0), (2, 2), (0, 0)))
    upward = speed_y > 0
    first_up = jnp.where(upward, padded[:, 1 : width_y + 1], padded[:, 3 : width_y + 3])
    second_up = jnp.where(upward, padded[:, 0:width_y], padded[:, 4 : width_y + 4])
    return jnp.abs(speed_y) * (1.5 * distribution - 2.0 * first_up + 0.5 * second_up)


def halo_pairs(size):
    up = [(i, i + 1) for i in range(size - 1)]
    down = [(j, i) for i, j in up]
    around = [(0, size - 1), (size - 1, 0)]
    return up, down, around


def advected(distribution, below, above, directions, wall_mask):
    tile_len, _, local_vel = distribution.shape
    moving, speed_x, speed_y = speeds(directions, lax.axis_index("vel") * local_vel, local_vel)
    padded_x = jnp.concatenate([below, distribution, above], axis=0)
    first_up = jnp.where(moving > 0, padded_x[1 : tile_len + 1], padded_x[3 : tile_len + 3])
    second_up = jnp.where(moving > 0, padded_x[0:tile_len], padded_x[4 : tile_len + 4])
    adv_x = speed_x * (1.5 * distribution - 2.0 * first_up + 0.5 * second_up)
    adv_y = transverse(distribution, speed_y)
    open_cells = (1 - wall_mask).astype(F32)[:, :, None]
    return open_cells, open_cells * (distribution - adv_x - adv_y)


def pieces_kernel(place, f_ref, keep_ref, send_ref, turned, *, cells, piece):
    chip, core = place[0], place[1]
    length = cells * piece
    peak = jnp.zeros((LANES, LANES), F32)
    for start in range(0, length, LANES):
        block = f_ref[:, start : start + LANES]
        peak = jnp.maximum(peak, jnp.abs(block))
        turned[start : start + LANES, :] = block.T.astype(BF16)
    top = jnp.max(peak, axis=(0, 1), keepdims=True) * 1.02 + 1e-30
    tail = jnp.broadcast_to(top, (TAIL, LANES)).astype(BF16)
    for q in range(cells // 2):
        other = chip ^ q
        for out, side in ((keep_ref, core), (send_ref, 1 - core)):
            at = pl.multiple_of((2 * other + side) * piece, TAIL)
            out[q, :piece, :] = turned[pl.ds(at, piece), :]
            out[q, piece:, :] = tail


def split_pieces(distribution, chip, core, cells):
    tile_len, width, local_vel = distribution.shape
    piece = local_vel // cells
    out = jax.ShapeDtypeStruct((cells // 2, piece + TAIL, LANES), BF16)
    return pl.pallas_call(
        functools.partial(pieces_kernel, cells=cells, piece=piece),
        out_shape=(out, out),
        in_specs=[pl.BlockSpec(memory_space=pltpu.SMEM), pl.BlockSpec(memory_space=pltpu.VMEM)],
        out_specs=(pl.BlockSpec(memory_space=pltpu.VMEM), pl.BlockSpec(memory_space=pltpu.VMEM)),
        scratch_shapes=[pltpu.VMEM((local_vel, LANES), BF16)],
        compiler_params=pltpu.CompilerParams(vmem_limit_bytes=24 << 20),
        cost_estimate=pl.CostEstimate(flops=local_vel * LANES, bytes_accessed=local_vel * LANES * 6, transcendentals=0),
        name="pieces",
    )(jnp.stack([chip, core]).astype(jnp.int32), distribution.reshape(tile_len * width, local_vel))


def product_kernel(vel, own, gx, gy, dx, dy, c_ref, keep_ref, send_ref, scale_ref, rows, lhs, *, piece, bound):
    slots = own.shape[0]

    @pl.when(pl.program_id(0) == 0)
    def _():
        for s in range(slots):
            for side in range(2):
                diagonal = dx if side == 0 else dy
                parts = ((0, own.at[s, side]), (1, gx.at[s, side]), (2, gy.at[s, side]), (3, diagonal.at[s]))
                top = jnp.zeros((TAIL, LANES), F32)
                for q, part in parts:
                    at = pl.multiple_of((vel[0] ^ q) * piece, TAIL)
                    rows[pl.ds(at, piece), :] = part[:piece, :]
                    top = jnp.maximum(top, part[piece:, :].astype(F32))
                lhs[(2 * s + side) * LANES : (2 * s + side + 1) * LANES, :] = rows[...].T
                scale_ref[s, side] = bound / top[:8, :]

    for s in range(slots):
        out = jnp.dot(lhs[2 * s * LANES : 2 * (s + 1) * LANES, :], c_ref[...], preferred_element_type=F32)
        keep_ref[s] = out[:LANES] * scale_ref[s, 0, 0:1, 0:1]
        send_ref[s] = out[LANES:] * scale_ref[s, 1, 0:1, 0:1]


def product(vel, own, gx, gy, dx, dy, matrix, block):
    slots = own.shape[0]
    piece = own.shape[2] - TAIL
    depth, columns = matrix.shape
    total = columns * 4
    whole = lambda a: pl.BlockSpec(a.shape, lambda n: (0,) * a.ndim)
    out = jax.ShapeDtypeStruct((slots, LANES, columns), F32)
    out_spec = pl.BlockSpec((slots, LANES, block), lambda n: (0, 0, n))
    return pl.pallas_call(
        functools.partial(product_kernel, piece=piece, bound=60000.0 / (total * COLLISION_MAX)),
        grid=(columns // block,),
        out_shape=(out, out, jax.ShapeDtypeStruct((slots, 2, 8, LANES), F32)),
        in_specs=[pl.BlockSpec(memory_space=pltpu.SMEM)]
        + [whole(a) for a in (own, gx, gy, dx, dy)]
        + [pl.BlockSpec((depth, block), lambda n: (0, n))],
        out_specs=(out_spec, out_spec, pl.BlockSpec((slots, 2, 8, LANES), lambda n: (0, 0, 0, 0))),
        scratch_shapes=[pltpu.VMEM((depth, LANES), BF16), pltpu.VMEM((slots * 2 * LANES, depth), BF16)],
        compiler_params=pltpu.CompilerParams(vmem_limit_bytes=40 << 20),
        cost_estimate=pl.CostEstimate(
            flops=2 * slots * 2 * LANES * depth * columns,
            bytes_accessed=depth * columns * 2 + slots * 2 * LANES * columns * 4,
            transcendentals=0,
        ),
        name="product",
    )(jnp.reshape(vel, (1,)).astype(jnp.int32), own, gx, gy, dx, dy, matrix)


def after(value, *earlier):
    return lax.optimization_barrier((value,) + earlier)[0]


def chain_body(distribution, collision, directions, wall_mask):
    tile_len, width, local_vel = distribution.shape
    cells = lax.axis_size("cell")
    cell = lax.axis_index("cell")
    vel = lax.axis_index("vel")
    chip, core = cell // 2, cell % 2
    matrix = collision.reshape(-1, local_vel)

    up, down, around = halo_pairs(cells)
    head, foot = distribution[:2], distribution[tile_len - 2 :]
    from_below = lax.ppermute(foot, "cell", up)
    from_above = lax.ppermute(head, "cell", down)

    other_core = [(i, i ^ 1) for i in range(cells)]
    across = lambda q: [(i, 2 * ((i // 2) ^ q) + i % 2) for i in range(cells)]
    in_x = [(i, i ^ 1) for i in range(4)]
    in_y = [(i, i ^ 2) for i in range(4)]
    chips = lambda *pairs: [(2 * a + c, 2 * b + c) for a, b in pairs for c in range(2)]
    ends = chips((0, 1), (3, 2))
    middle = chips((1, 2), (2, 1))
    outward = chips((2, 3), (1, 0))

    keep, send = split_pieces(distribution, chip, core, cells)
    got = lax.ppermute(send, "cell", other_core)
    both = [jnp.stack([keep[q], got[q]])[None] for q in range(4)]

    def gathered(own):
        gx = lax.ppermute(own, "vel", in_x)
        gy = lax.ppermute(own, "vel", in_y)
        dx = lax.ppermute(gx[:, 0], "vel", in_y)
        dy = lax.ppermute(gy[:, 1], "vel", in_x)
        return own, gx, gy, dx, dy

    def partial(parts):
        mine, theirs, scale = product(vel, *parts, matrix, 384)
        return mine, lax.ppermute(theirs, "cell", other_core), scale

    z3 = lax.ppermute(both[3], "cell", across(3))
    g0 = gathered(both[0])
    z2 = lax.ppermute(after(both[2], z3), "cell", across(2))
    z1 = lax.ppermute(after(both[1], z3), "cell", across(1))
    g3 = gathered(z3)
    wrapping = jnp.where(cell == 0, head, foot)
    from_around = lax.ppermute(after(wrapping, z2, z1), "cell", around)
    mine3, theirs3, _ = partial(g3)
    p3 = (mine3 + theirs3)[0]
    a0 = lax.ppermute(p3.astype(F16), "cell", ends)
    g2 = gathered(after(z2, g3[3], g3[4]))
    mine2, theirs2, _ = partial(g2)
    p2 = (mine2 + theirs2)[0]
    a1 = lax.ppermute(after(p2.astype(F16), a0), "cell", ends)
    b1 = lax.ppermute((p2 + a0.astype(F32)).astype(F16), "cell", middle)
    g1 = gathered(after(z1, g2[3], g2[4]))
    mine1, theirs1, _ = partial(g1)
    p1 = (mine1 + theirs1)[0]
    a2 = lax.ppermute(after(p1.astype(F16), a1), "cell", ends)
    b2 = lax.ppermute((p3 + a1.astype(F32)).astype(F16), "cell", middle)
    c2 = lax.ppermute((p1 + b1.astype(F32)).astype(F16), "cell", outward)
    mine0, theirs0, scale = partial(g0)

    below = jnp.where(cell == 0, from_around, from_below)
    above = jnp.where(cell == cells - 1, from_around, from_above)
    open_cells, base = advected(distribution, below, above, directions, wall_mask)
    shape = distribution.shape
    rest = (mine0 + theirs0).reshape(shape)
    arrived = (a2.astype(F32) + b2.astype(F32) + c2.astype(F32)).reshape(shape)
    return base + open_cells * (relax / scale[0, 0, 0, 0]) * (rest + arrived)


def plain_body(distribution, collision, directions, wall_mask):
    tile_len, width, local_vel = distribution.shape
    cells = lax.axis_size("cell")
    vels = lax.axis_size("vel")
    cell = lax.axis_index("cell")
    piece = local_vel // cells
    up, down, around = halo_pairs(cells)
    head, foot = distribution[:2], distribution[tile_len - 2 :]
    from_around = lax.ppermute(jnp.where(cell == 0, head, foot), "cell", around)
    below = jnp.where(cell == 0, from_around, lax.ppermute(foot, "cell", up))
    above = jnp.where(cell == cells - 1, from_around, lax.ppermute(head, "cell", down))
    open_cells, base = advected(distribution, below, above, directions, wall_mask)
    pieces = distribution.astype(BF16).reshape(tile_len * width, cells, piece)
    spread = lax.all_to_all(pieces, "cell", split_axis=1, concat_axis=0, tiled=True)
    panel = lax.all_gather(spread.reshape(-1, piece), "vel", axis=1, tiled=True)
    part = jnp.dot(panel, collision.reshape(vels * piece, local_vel), preferred_element_type=F32)
    gain = lax.psum_scatter(part, "cell", scatter_dimension=0, tiled=True)
    return base + open_cells * relax * gain.reshape(distribution.shape)


def body(distribution, collision, directions, wall_mask):
    tile_len, width, local_vel = distribution.shape
    cells = lax.axis_size("cell")
    piece = local_vel // cells
    fits = tile_len * width == LANES and piece % TAIL == 0 and local_vel % (3 * LANES) == 0
    if cells == 8 and lax.axis_size("vel") == 4 and fits:
        return chain_body(distribution, collision, directions, wall_mask)
    return plain_body(distribution, collision, directions, wall_mask)


def solution(mesh):
    in_specs = (P("cell", None, "vel"), P(None, "cell", None, "vel"), P("vel"), P("cell", None))
    out_specs = P("cell", None, "vel")
    return jax.shard_map(body, mesh=mesh, in_specs=in_specs, out_specs=out_specs, check_vma=False)
```

```python
import functools

import jax
import jax.numpy as jnp
from jax import lax
from jax.experimental import pallas as pl
from jax.experimental.pallas import tpu as pltpu
from jax.sharding import PartitionSpec as P

VG = 24
courant = 0.8
relax = 0.5
COLLISION_MAX = 0.0546875
TAIL = 16
LANES = 128
BF16 = jnp.bfloat16
F16 = jnp.float16
F32 = jnp.float32
HALF_MAX = 60000.0


def speeds(directions, offset, length):
    vel_index = offset + jnp.arange(length, dtype=jnp.int32)
    grid_x = vel_index // (VG * VG)
    grid_y = vel_index // VG % VG
    moving = 2 * directions - 1
    speed_x = courant * (grid_x.astype(F32) + 0.5) / VG
    speed_y = courant * (grid_y.astype(F32) - 0.5 * (VG - 1)) / VG
    return (moving, speed_x, speed_y)


def transverse(distribution, speed_y):
    width_y = distribution.shape[1]
    padded = jnp.pad(distribution, ((0, 0), (2, 2), (0, 0)))
    upward = speed_y > 0
    first_up = jnp.where(upward, padded[:, 1 : width_y + 1], padded[:, 3 : width_y + 3])
    second_up = jnp.where(upward, padded[:, 0:width_y], padded[:, 4 : width_y + 4])
    return jnp.abs(speed_y) * (1.5 * distribution - 2.0 * first_up + 0.5 * second_up)


def halo_pairs(size):
    up = [(i, i + 1) for i in range(size - 1)]
    down = [(j, i) for i, j in up]
    around = [(0, size - 1), (size - 1, 0)]
    return up, down, around


def advected(distribution, below, above, directions, wall_mask, offset):
    tile_len, _, local_vel = distribution.shape
    moving, speed_x, speed_y = speeds(directions, offset, local_vel)
    padded_x = jnp.concatenate([below, distribution, above], axis=0)
    first_up = jnp.where(moving > 0, padded_x[1 : tile_len + 1], padded_x[3 : tile_len + 3])
    second_up = jnp.where(moving > 0, padded_x[0:tile_len], padded_x[4 : tile_len + 4])
    adv_x = speed_x * (1.5 * distribution - 2.0 * first_up + 0.5 * second_up)
    adv_y = transverse(distribution, speed_y)
    open_cells = (1 - wall_mask).astype(F32)[:, :, None]
    return open_cells, open_cells * (distribution - adv_x - adv_y)


def pieces_kernel(place, f_ref, keep_ref, send_ref, turned, *, cells, piece):
    chip, core = place[0], place[1]
    length = cells * piece
    peak = jnp.zeros((LANES, LANES), F32)
    for start in range(0, length, LANES):
        block = f_ref[:, start : start + LANES]
        peak = jnp.maximum(peak, jnp.abs(block))
        turned[start : start + LANES, :] = block.T.astype(BF16)
    top = jnp.max(peak, axis=(0, 1), keepdims=True) * 1.02 + 1e-30
    tail = jnp.broadcast_to(top, (TAIL, LANES)).astype(BF16)
    for q in range(cells // 2):
        other = chip ^ q
        for out, side in ((keep_ref, core), (send_ref, 1 - core)):
            at = pl.multiple_of((2 * other + side) * piece, TAIL)
            out[q, :piece, :] = turned[pl.ds(at, piece), :]
            out[q, piece:, :] = tail


def split_pieces(distribution, place, cells):
    tile_len, width, local_vel = distribution.shape
    piece = local_vel // cells
    out = jax.ShapeDtypeStruct((cells // 2, piece + TAIL, LANES), BF16)
    return pl.pallas_call(
        functools.partial(pieces_kernel, cells=cells, piece=piece),
        out_shape=(out, out),
        in_specs=[pl.BlockSpec(memory_space=pltpu.SMEM), pl.BlockSpec(memory_space=pltpu.VMEM)],
        out_specs=(pl.BlockSpec(memory_space=pltpu.VMEM), pl.BlockSpec(memory_space=pltpu.VMEM)),
        scratch_shapes=[pltpu.VMEM((local_vel, LANES), BF16)],
        compiler_params=pltpu.CompilerParams(vmem_limit_bytes=10 << 20),
        cost_estimate=pl.CostEstimate(flops=local_vel * LANES, bytes_accessed=local_vel * LANES * 6, transcendentals=0),
        name="pieces",
    )(place, distribution.reshape(tile_len * width, local_vel))


def product_kernel(place, own, gx, gy, dx, dy, c_ref, keep_ref, send_ref, scale_ref, rows, lhs, *, piece, bound):
    slots = own.shape[0]

    @pl.when(pl.program_id(0) == 0)
    def _():
        for s in range(slots):
            for side in range(2):
                diagonal = dx if side == 0 else dy
                parts = ((0, own.at[s, side]), (1, gx.at[s, side]), (2, gy.at[s, side]), (3, diagonal.at[s]))
                top = jnp.zeros((TAIL, LANES), F32)
                for q, part in parts:
                    at = pl.multiple_of((place[2] ^ q) * piece, TAIL)
                    rows[pl.ds(at, piece), :] = part[:piece, :]
                    top = jnp.maximum(top, part[piece:, :].astype(F32))
                lhs[(2 * s + side) * LANES : (2 * s + side + 1) * LANES, :] = rows[...].T
                scale_ref[s, side] = bound / top[:8, :]

    for s in range(slots):
        out = jnp.dot(lhs[2 * s * LANES : 2 * (s + 1) * LANES, :], c_ref[...], preferred_element_type=F32)
        keep_ref[s] = out[:LANES] * scale_ref[s, 0, 0:1, 0:1]
        send_ref[s] = out[LANES:] * scale_ref[s, 1, 0:1, 0:1]


def product(place, own, gx, gy, dx, dy, matrix, vels):
    slots = own.shape[0]
    piece = own.shape[2] - TAIL
    depth, columns = matrix.shape
    block = columns // 3
    whole = lambda a: pl.BlockSpec(a.shape, lambda n: (0,) * a.ndim)
    out = jax.ShapeDtypeStruct((slots, LANES, columns), F32)
    out_spec = pl.BlockSpec((slots, LANES, block), lambda n: (0, 0, n))
    return pl.pallas_call(
        functools.partial(product_kernel, piece=piece, bound=HALF_MAX / (vels * columns * COLLISION_MAX)),
        grid=(columns // block,),
        out_shape=(out, out, jax.ShapeDtypeStruct((slots, 2, 8, LANES), F32)),
        in_specs=[pl.BlockSpec(memory_space=pltpu.SMEM)]
        + [whole(a) for a in (own, gx, gy, dx, dy)]
        + [pl.BlockSpec((depth, block), lambda n: (0, n))],
        out_specs=(out_spec, out_spec, pl.BlockSpec((slots, 2, 8, LANES), lambda n: (0, 0, 0, 0))),
        scratch_shapes=[pltpu.VMEM((depth, LANES), BF16), pltpu.VMEM((slots * 2 * LANES, depth), BF16)],
        compiler_params=pltpu.CompilerParams(vmem_limit_bytes=18 << 20),
        cost_estimate=pl.CostEstimate(
            flops=2 * slots * 2 * LANES * depth * columns,
            bytes_accessed=depth * columns * 2 + slots * 2 * LANES * columns * 4,
            transcendentals=0,
        ),
        name="product",
    )(place, own, gx, gy, dx, dy, matrix)


def edge_kernel(place, a_ref, c_ref, d_ref, out_ref, *, cells):
    chip, core = place[0], place[1]
    cell = 2 * chip + core
    last = cells // 2 - 1
    is_end = jnp.logical_or(chip == 0, chip == last)
    held = ((a_ref, jnp.where(is_end, 3, 0)), (c_ref, jnp.where(is_end, 1, 3)), (d_ref, jnp.where(is_end, 0, 1)))
    for k, other in enumerate(((cell + cells - 1) % cells, (cell + 1) % cells)):
        total = jnp.zeros((TAIL, LANES), F32)
        for ref, q in held:
            for side in range(2):
                here = jnp.logical_and((other // 2) ^ chip == q, (other % 2) ^ core == side)
                tail = ref[0, side, ref.shape[2] - TAIL :, :].astype(F32)
                total = total + jnp.where(here, tail, jnp.zeros_like(tail))
        out_ref[k] = total[:8] * (1.0 / HALF_MAX)


def edge_scales(place, a, c, d, cells):
    vmem = pl.BlockSpec(memory_space=pltpu.VMEM)
    return pl.pallas_call(
        functools.partial(edge_kernel, cells=cells),
        out_shape=jax.ShapeDtypeStruct((2, 8, LANES), F32),
        in_specs=[pl.BlockSpec(memory_space=pltpu.SMEM), vmem, vmem, vmem],
        out_specs=vmem,
        compiler_params=pltpu.CompilerParams(vmem_limit_bytes=4 << 20),
        cost_estimate=pl.CostEstimate(flops=10000, bytes_accessed=10000, transcendentals=0),
        name="edges",
    )(place, a, c, d)


def after(value, *earlier):
    return lax.optimization_barrier((value,) + earlier)[0]


def chain_body(distribution, collision, directions, wall_mask):
    tile_len, width, local_vel = distribution.shape
    cells = lax.axis_size("cell")
    cell = lax.axis_index("cell")
    vel = lax.axis_index("vel")
    place = jnp.stack([cell >> 1, cell & 1, vel])
    is_end = jnp.logical_or(cell < 2, cell >= cells - 2)
    distribution, place, is_end, offset = lax.optimization_barrier((distribution, place, is_end, vel * local_vel))
    matrix = pltpu.with_memory_space_constraint(collision.reshape(-1, local_vel), pltpu.HBM)

    other_core = [(i, i ^ 1) for i in range(cells)]
    across = lambda q: [(i, 2 * ((i // 2) ^ q) + i % 2) for i in range(cells)]
    in_x = [(i, i ^ 1) for i in range(4)]
    in_y = [(i, i ^ 2) for i in range(4)]
    chips = lambda *pairs: [(2 * a + c, 2 * b + c) for a, b in pairs for c in range(2)]
    ends = chips((0, 1), (3, 2))
    middle = chips((1, 2), (2, 1))
    outward = chips((2, 3), (1, 0))
    ring = [(i, (i + 1) % cells) for i in range(cells)]

    def gather_x_y(own):
        return own, lax.ppermute(own, "vel", in_x), lax.ppermute(own, "vel", in_y)

    def gather_diagonal(parts, *earlier):
        own, gx, gy = parts
        dx = lax.ppermute(after(gx[:, 0], *earlier), "vel", in_y)
        dy = lax.ppermute(after(gy[:, 1], *earlier), "vel", in_x)
        return own, gx, gy, dx, dy

    def exchanged(mine, theirs):
        theirs = lax.ppermute(theirs.astype(F16), "cell", other_core)
        return [mine[s] + theirs[s].astype(F32) for s in range(mine.shape[0])]

    def behind(parts, *earlier):
        return (after(parts[0], *earlier),) + tuple(parts[1:])

    keep, send = split_pieces(distribution, place, cells)
    got = lax.ppermute(send, "cell", other_core)
    both = [jnp.stack([keep[q], got[q]])[None] for q in range(4)]

    from_end = lax.ppermute(both[3], "cell", chips((0, 3), (3, 0)))
    slot_a = jnp.where(is_end, from_end, both[0])
    ga = gather_x_y(slot_a)
    slot_b = lax.ppermute(after(both[2], from_end), "cell", across(2))
    z1 = lax.ppermute(after(both[1], from_end), "cell", across(1))
    from_middle = lax.ppermute(after(both[3], from_end), "cell", middle)
    ga = gather_diagonal(ga)
    own_top = keep[0:1, keep.shape[1] - 1 :, 0:1].astype(F32)
    edges = after(distribution, slot_b, z1, from_middle) * (HALF_MAX / own_top)
    from_below = lax.ppermute(edges[tile_len - 2 :].astype(F16), "cell", ring)
    from_above = lax.ppermute(edges[:2].astype(F16), "cell", [(j, i) for i, j in ring])

    mine_a, theirs_a, scale_a = product(place, *behind(ga, slot_b), matrix, 4)
    gb = gather_x_y(after(slot_b, theirs_a))
    (pa,) = exchanged(mine_a, theirs_a)
    ma = after(pa.astype(F16), from_below, from_above)
    a0 = lax.ppermute(ma, "cell", ends)
    gb = gather_diagonal(gb, ma)
    mine_b, theirs_b, _ = product(place, *behind(gb, ma), matrix, 4)
    z1, from_middle, both0, _ = lax.optimization_barrier((z1, from_middle, both[0], theirs_b))
    slot_c = jnp.where(is_end, z1, from_middle)
    slot_d = jnp.where(is_end, both0, z1)
    gcd = gather_x_y(jnp.concatenate([slot_c, slot_d]))
    (pb,) = exchanged(mine_b, theirs_b)
    mb = pb.astype(F16)
    a1 = lax.ppermute(after(mb, a0), "cell", ends)
    b1 = lax.ppermute((pb + a0.astype(F32)).astype(F16), "cell", middle)
    gcd = gather_diagonal(gcd, mb)
    mine_cd, theirs_cd, scale_cd = product(place, *behind(gcd, mb), matrix, 4)
    pc, pd = exchanged(mine_cd, theirs_cd)
    a2 = lax.ppermute(after(pc.astype(F16), a1), "cell", ends)
    b2 = lax.ppermute((pc + a1.astype(F32)).astype(F16), "cell", middle)
    c2 = lax.ppermute((pd + b1.astype(F32)).astype(F16), "cell", outward)

    edge = edge_scales(place, *lax.optimization_barrier((slot_a, slot_c, slot_d, mb))[:3], cells)
    below = from_below.astype(F32) * edge[0:1, :1, :1]
    above = from_above.astype(F32) * edge[1:2, :1, :1]
    open_cells, base = advected(after(distribution, mb), below, above, directions, wall_mask, offset)
    scale = jnp.where(is_end, scale_cd[1, 0:1, :1, :1], scale_a[0, 0:1, :1, :1])
    own = jnp.where(is_end, pd, pa)
    factor = open_cells * (relax / scale)
    base, factor, own = lax.optimization_barrier((base, factor, own))
    arrived = a2.astype(F32) + b2.astype(F32) + c2.astype(F32)
    return base + factor * (own + arrived).reshape(distribution.shape)


def plain_body(distribution, collision, directions, wall_mask):
    tile_len, width, local_vel = distribution.shape
    cells = lax.axis_size("cell")
    vels = lax.axis_size("vel")
    cell = lax.axis_index("cell")
    piece = local_vel // cells
    up, down, around = halo_pairs(cells)
    head, foot = distribution[:2], distribution[tile_len - 2 :]
    from_around = lax.ppermute(jnp.where(cell == 0, head, foot), "cell", around)
    below = jnp.where(cell == 0, from_around, lax.ppermute(foot, "cell", up))
    above = jnp.where(cell == cells - 1, from_around, lax.ppermute(head, "cell", down))
    offset = lax.axis_index("vel") * local_vel
    open_cells, base = advected(distribution, below, above, directions, wall_mask, offset)
    pieces = distribution.astype(BF16).reshape(tile_len * width, cells, piece)
    spread = lax.all_to_all(pieces, "cell", split_axis=1, concat_axis=0, tiled=True)
    panel = lax.all_gather(spread.reshape(-1, piece), "vel", axis=1, tiled=True)
    part = jnp.dot(panel, collision.reshape(vels * piece, local_vel), preferred_element_type=F32)
    gain = lax.psum_scatter(part, "cell", scatter_dimension=0, tiled=True)
    return base + open_cells * relax * gain.reshape(distribution.shape)


def body(distribution, collision, directions, wall_mask):
    tile_len, width, local_vel = distribution.shape
    cells = lax.axis_size("cell")
    piece = local_vel // cells
    fits = tile_len * width == LANES and piece % TAIL == 0 and local_vel % (3 * LANES) == 0
    if cells == 8 and lax.axis_size("vel") == 4 and fits:
        return chain_body(distribution, collision, directions, wall_mask)
    return plain_body(distribution, collision, directions, wall_mask)


def solution(mesh):
    in_specs = (P("cell", None, "vel"), P(None, "cell", None, "vel"), P("vel"), P("cell", None))
    out_specs = P("cell", None, "vel")
    return jax.shard_map(body, mesh=mesh, in_specs=in_specs, out_specs=out_specs, check_vma=False)
```

```python
import functools

import jax
import jax.numpy as jnp
from jax import lax
from jax.experimental import pallas as pl
from jax.experimental.pallas import tpu as pltpu
from jax.sharding import PartitionSpec as P

VG = 24
courant = 0.8
relax = 0.5
COLLISION_MAX = 0.0546875
TAIL = 16
LANES = 128
BF16 = jnp.bfloat16
F16 = jnp.float16
F32 = jnp.float32
HALF_MAX = 60000.0


def speeds(directions, offset, length):
    vel_index = offset + jnp.arange(length, dtype=jnp.int32)
    grid_x = vel_index // (VG * VG)
    grid_y = vel_index // VG % VG
    moving = 2 * directions - 1
    speed_x = courant * (grid_x.astype(F32) + 0.5) / VG
    speed_y = courant * (grid_y.astype(F32) - 0.5 * (VG - 1)) / VG
    return (moving, speed_x, speed_y)


def transverse(distribution, speed_y):
    width_y = distribution.shape[1]
    padded = jnp.pad(distribution, ((0, 0), (2, 2), (0, 0)))
    upward = speed_y > 0
    first_up = jnp.where(upward, padded[:, 1 : width_y + 1], padded[:, 3 : width_y + 3])
    second_up = jnp.where(upward, padded[:, 0:width_y], padded[:, 4 : width_y + 4])
    return jnp.abs(speed_y) * (1.5 * distribution - 2.0 * first_up + 0.5 * second_up)


def halo_pairs(size):
    up = [(i, i + 1) for i in range(size - 1)]
    down = [(j, i) for i, j in up]
    around = [(0, size - 1), (size - 1, 0)]
    return up, down, around


def advected(distribution, below, above, directions, wall_mask, offset):
    tile_len, _, local_vel = distribution.shape
    moving, speed_x, speed_y = speeds(directions, offset, local_vel)
    padded_x = jnp.concatenate([below, distribution, above], axis=0)
    first_up = jnp.where(moving > 0, padded_x[1 : tile_len + 1], padded_x[3 : tile_len + 3])
    second_up = jnp.where(moving > 0, padded_x[0:tile_len], padded_x[4 : tile_len + 4])
    adv_x = speed_x * (1.5 * distribution - 2.0 * first_up + 0.5 * second_up)
    adv_y = transverse(distribution, speed_y)
    open_cells = (1 - wall_mask).astype(F32)[:, :, None]
    return open_cells, open_cells * (distribution - adv_x - adv_y)


def pieces_kernel(place, f_ref, keep_ref, send_ref, turned, *, cells, piece):
    chip, core = place[0], place[1]
    length = cells * piece
    peak = jnp.zeros((LANES, LANES), F32)
    for start in range(0, length, LANES):
        block = f_ref[:, start : start + LANES]
        peak = jnp.maximum(peak, jnp.abs(block))
        turned[start : start + LANES, :] = block.T.astype(BF16)
    top = jnp.max(peak, axis=(0, 1), keepdims=True) * 1.02 + 1e-30
    tail = jnp.broadcast_to(top, (TAIL, LANES)).astype(BF16)
    for q in range(cells // 2):
        other = chip ^ q
        for out, side in ((keep_ref, core), (send_ref, 1 - core)):
            at = pl.multiple_of((2 * other + side) * piece, TAIL)
            out[q, :piece, :] = turned[pl.ds(at, piece), :]
            out[q, piece:, :] = tail


def split_pieces(distribution, place, cells):
    tile_len, width, local_vel = distribution.shape
    piece = local_vel // cells
    out = jax.ShapeDtypeStruct((cells // 2, piece + TAIL, LANES), BF16)
    return pl.pallas_call(
        functools.partial(pieces_kernel, cells=cells, piece=piece),
        out_shape=(out, out),
        in_specs=[pl.BlockSpec(memory_space=pltpu.SMEM), pl.BlockSpec(memory_space=pltpu.VMEM)],
        out_specs=(pl.BlockSpec(memory_space=pltpu.VMEM), pl.BlockSpec(memory_space=pltpu.VMEM)),
        scratch_shapes=[pltpu.VMEM((local_vel, LANES), BF16)],
        compiler_params=pltpu.CompilerParams(vmem_limit_bytes=10 << 20),
        cost_estimate=pl.CostEstimate(flops=local_vel * LANES, bytes_accessed=local_vel * LANES * 6, transcendentals=0),
        name="pieces",
    )(place, distribution.reshape(tile_len * width, local_vel))


def product_kernel(place, own, gx, gy, dx, dy, c_ref, keep_ref, send_ref, scale_ref, rows, lhs, *, piece, bound):
    slots = own.shape[0]

    @pl.when(place[2] >= 0)
    def _():
        for s in range(slots):
            for side in range(2):
                diagonal = dx if side == 0 else dy
                parts = ((0, own.at[s, side]), (1, gx.at[s, side]), (2, gy.at[s, side]), (3, diagonal.at[s]))
                top = jnp.zeros((TAIL, LANES), F32)
                for q, part in parts:
                    at = pl.multiple_of((place[2] ^ q) * piece, TAIL)
                    rows[2 * s + side, pl.ds(at, piece), :] = part[:piece, :]
                    top = jnp.maximum(top, part[piece:, :].astype(F32))
                scale_ref[s, side] = bound / top[:8, :]

    @pl.when(place[1] >= 0)
    def _():
        for k in range(2 * slots):
            lhs[k * LANES : (k + 1) * LANES, :] = rows[k].T

    for s in range(slots):
        out = jnp.dot(lhs[2 * s * LANES : 2 * (s + 1) * LANES, :], c_ref[...], preferred_element_type=F32)
        keep_ref[s] = out[:LANES] * scale_ref[s, 0, 0:1, 0:1]
        send_ref[s] = out[LANES:] * scale_ref[s, 1, 0:1, 0:1]


def product(place, own, gx, gy, dx, dy, matrix, vels):
    slots = own.shape[0]
    piece = own.shape[2] - TAIL
    depth, columns = matrix.shape
    out = jax.ShapeDtypeStruct((slots, LANES, columns), F32)
    vmem = pl.BlockSpec(memory_space=pltpu.VMEM)
    return pl.pallas_call(
        functools.partial(product_kernel, piece=piece, bound=HALF_MAX / (vels * columns * COLLISION_MAX)),
        out_shape=(out, out, jax.ShapeDtypeStruct((slots, 2, 8, LANES), F32)),
        in_specs=[pl.BlockSpec(memory_space=pltpu.SMEM)] + [vmem] * 6,
        out_specs=(vmem, vmem, vmem),
        scratch_shapes=[pltpu.VMEM((2 * slots, depth, LANES), BF16), pltpu.VMEM((slots * 2 * LANES, depth), BF16)],
        compiler_params=pltpu.CompilerParams(vmem_limit_bytes=8 << 20),
        cost_estimate=pl.CostEstimate(
            flops=2 * slots * 2 * LANES * depth * columns,
            bytes_accessed=depth * columns * 2 + slots * 2 * LANES * columns * 4,
            transcendentals=0,
        ),
        name="product",
    )(place, own, gx, gy, dx, dy, matrix)


def load_kernel(c_ref, out_ref, sem):
    copy = pltpu.make_async_copy(c_ref, out_ref, sem)
    copy.start()
    copy.wait()


def loaded(matrix):
    return pl.pallas_call(
        load_kernel,
        out_shape=jax.ShapeDtypeStruct(matrix.shape, matrix.dtype),
        in_specs=[pl.BlockSpec(memory_space=pltpu.HBM)],
        out_specs=pl.BlockSpec(memory_space=pltpu.VMEM),
        scratch_shapes=[pltpu.SemaphoreType.DMA],
        compiler_params=pltpu.CompilerParams(vmem_limit_bytes=1 << 20),
        cost_estimate=pl.CostEstimate(flops=1, bytes_accessed=2 * matrix.size * 2, transcendentals=0),
        name="load",
    )(matrix)


def edge_kernel(place, a_ref, c_ref, d_ref, out_ref, *, cells):
    chip, core = place[0], place[1]
    cell = 2 * chip + core
    last = cells // 2 - 1
    is_end = jnp.logical_or(chip == 0, chip == last)
    held = ((a_ref, jnp.where(is_end, 3, 0)), (c_ref, jnp.where(is_end, 1, 3)), (d_ref, jnp.where(is_end, 0, 1)))
    for k, other in enumerate(((cell + cells - 1) % cells, (cell + 1) % cells)):
        total = jnp.zeros((TAIL, LANES), F32)
        for ref, q in held:
            for side in range(2):
                here = jnp.logical_and((other // 2) ^ chip == q, (other % 2) ^ core == side)
                tail = ref[0, side, ref.shape[2] - TAIL :, :].astype(F32)
                total = total + jnp.where(here, tail, jnp.zeros_like(tail))
        out_ref[k] = total[:8] * (1.0 / HALF_MAX)


def edge_scales(place, a, c, d, cells):
    vmem = pl.BlockSpec(memory_space=pltpu.VMEM)
    return pl.pallas_call(
        functools.partial(edge_kernel, cells=cells),
        out_shape=jax.ShapeDtypeStruct((2, 8, LANES), F32),
        in_specs=[pl.BlockSpec(memory_space=pltpu.SMEM), vmem, vmem, vmem],
        out_specs=vmem,
        compiler_params=pltpu.CompilerParams(vmem_limit_bytes=4 << 20),
        cost_estimate=pl.CostEstimate(flops=10000, bytes_accessed=10000, transcendentals=0),
        name="edges",
    )(place, a, c, d)


def after(value, *earlier):
    return lax.optimization_barrier((value,) + earlier)[0]


def chain_body(distribution, collision, directions, wall_mask):
    tile_len, width, local_vel = distribution.shape
    cells = lax.axis_size("cell")
    cell = lax.axis_index("cell")
    vel = lax.axis_index("vel")
    place = jnp.stack([cell >> 1, cell & 1, vel])
    is_end = jnp.logical_or(cell < 2, cell >= cells - 2)
    distribution, place, is_end, offset = lax.optimization_barrier((distribution, place, is_end, vel * local_vel))
    matrix = collision.reshape(-1, local_vel)

    other_core = [(i, i ^ 1) for i in range(cells)]
    across = lambda q: [(i, 2 * ((i // 2) ^ q) + i % 2) for i in range(cells)]
    in_x = [(i, i ^ 1) for i in range(4)]
    in_y = [(i, i ^ 2) for i in range(4)]
    chips = lambda *pairs: [(2 * a + c, 2 * b + c) for a, b in pairs for c in range(2)]
    ends = chips((0, 1), (3, 2))
    middle = chips((1, 2), (2, 1))
    outward = chips((2, 3), (1, 0))
    ring = [(i, (i + 1) % cells) for i in range(cells)]

    def gather_x_y(own):
        return own, lax.ppermute(own, "vel", in_x), lax.ppermute(own, "vel", in_y)

    def gather_diagonal(parts, *earlier):
        own, gx, gy = parts
        dx = lax.ppermute(after(gx[:, 0], *earlier), "vel", in_y)
        dy = lax.ppermute(after(gy[:, 1], *earlier), "vel", in_x)
        return own, gx, gy, dx, dy

    def exchanged(mine, theirs):
        theirs = lax.ppermute(theirs.astype(F16), "cell", other_core)
        return [mine[s] + theirs[s].astype(F32) for s in range(mine.shape[0])]

    def behind(parts, *earlier):
        return (after(parts[0], *earlier),) + tuple(parts[1:])

    keep, send = split_pieces(distribution, place, cells)
    got = lax.ppermute(send, "cell", other_core)
    matrix = loaded(pltpu.with_memory_space_constraint(after(matrix, got), pltpu.HBM))
    both = [jnp.stack([keep[q], got[q]])[None] for q in range(4)]

    from_end = lax.ppermute(both[3], "cell", chips((0, 3), (3, 0)))
    ga = gather_x_y(jnp.where(is_end, from_end, both[0]))
    slot_a = ga[0]
    own_top = keep[0:1, keep.shape[1] - 1 :, 0:1].astype(F32)
    edges = after(distribution, from_end) * (HALF_MAX / own_top)
    from_below = lax.ppermute(edges[tile_len - 2 :].astype(F16), "cell", ring)
    from_above = lax.ppermute(edges[:2].astype(F16), "cell", [(j, i) for i, j in ring])
    ga = gather_diagonal(ga)
    mine_a, theirs_a, scale_a = product(place, *ga, matrix, 4)
    theirs_a, both1, both2, both3, from_below, from_above = lax.optimization_barrier(
        (theirs_a, both[1], both[2], both[3], from_below, from_above)
    )
    slot_b = lax.ppermute(both2, "cell", across(2))
    z1 = lax.ppermute(both1, "cell", across(1))
    from_middle = lax.ppermute(both3, "cell", middle)
    (pa,) = exchanged(mine_a, theirs_a)
    ma, slot_b, z1, from_middle = lax.optimization_barrier((pa.astype(F16), slot_b, z1, from_middle))
    a0 = lax.ppermute(ma, "cell", ends)
    gb = gather_x_y(slot_b)
    gb = gather_diagonal(gb)
    mine_b, theirs_b, _ = product(place, *gb, matrix, 4)
    (pb,) = exchanged(mine_b, theirs_b)
    mb = pb.astype(F16)
    a1 = lax.ppermute(after(mb, a0), "cell", ends)
    b1 = lax.ppermute((pb + a0.astype(F32)).astype(F16), "cell", middle)
    z1, from_middle, both0, _ = lax.optimization_barrier((z1, from_middle, both[0], a0))
    slot_c = jnp.where(is_end, z1, from_middle)
    slot_d = jnp.where(is_end, both0, z1)
    gcd = gather_x_y(jnp.concatenate([slot_c, slot_d]))
    gcd = gather_diagonal(gcd, mb)
    mine_cd, theirs_cd, scale_cd = product(place, *behind(gcd, mb), matrix, 4)
    pc, pd = exchanged(mine_cd, theirs_cd)
    a2 = lax.ppermute(after(pc.astype(F16), a1), "cell", ends)
    b2 = lax.ppermute((pc + a1.astype(F32)).astype(F16), "cell", middle)
    c2 = lax.ppermute((pd + b1.astype(F32)).astype(F16), "cell", outward)

    edge = edge_scales(place, *lax.optimization_barrier((slot_a, slot_c, slot_d, mb))[:3], cells)
    below = from_below.astype(F32) * edge[0:1, :1, :1]
    above = from_above.astype(F32) * edge[1:2, :1, :1]
    open_cells, base = advected(after(distribution, mb), below, above, directions, wall_mask, offset)
    scale = jnp.where(is_end, scale_cd[1, 0:1, :1, :1], scale_a[0, 0:1, :1, :1])
    own = jnp.where(is_end, pd, pa)
    factor = open_cells * (relax / scale)
    base, factor, own = lax.optimization_barrier((base, factor, own))
    arrived = a2.astype(F32) + b2.astype(F32) + c2.astype(F32)
    return base + factor * (own + arrived).reshape(distribution.shape)


def plain_body(distribution, collision, directions, wall_mask):
    tile_len, width, local_vel = distribution.shape
    cells = lax.axis_size("cell")
    vels = lax.axis_size("vel")
    cell = lax.axis_index("cell")
    piece = local_vel // cells
    up, down, around = halo_pairs(cells)
    head, foot = distribution[:2], distribution[tile_len - 2 :]
    from_around = lax.ppermute(jnp.where(cell == 0, head, foot), "cell", around)
    below = jnp.where(cell == 0, from_around, lax.ppermute(foot, "cell", up))
    above = jnp.where(cell == cells - 1, from_around, lax.ppermute(head, "cell", down))
    offset = lax.axis_index("vel") * local_vel
    open_cells, base = advected(distribution, below, above, directions, wall_mask, offset)
    pieces = distribution.astype(BF16).reshape(tile_len * width, cells, piece)
    spread = lax.all_to_all(pieces, "cell", split_axis=1, concat_axis=0, tiled=True)
    panel = lax.all_gather(spread.reshape(-1, piece), "vel", axis=1, tiled=True)
    part = jnp.dot(panel, collision.reshape(vels * piece, local_vel), preferred_element_type=F32)
    gain = lax.psum_scatter(part, "cell", scatter_dimension=0, tiled=True)
    return base + open_cells * relax * gain.reshape(distribution.shape)


def body(distribution, collision, directions, wall_mask):
    tile_len, width, local_vel = distribution.shape
    cells = lax.axis_size("cell")
    piece = local_vel // cells
    fits = tile_len * width == LANES and piece % TAIL == 0 and local_vel % (3 * LANES) == 0
    if cells == 8 and lax.axis_size("vel") == 4 and fits:
        return chain_body(distribution, collision, directions, wall_mask)
    return plain_body(distribution, collision, directions, wall_mask)


def solution(mesh):
    in_specs = (P("cell", None, "vel"), P(None, "cell", None, "vel"), P("vel"), P("cell", None))
    out_specs = P("cell", None, "vel")
    return jax.shard_map(body, mesh=mesh, in_specs=in_specs, out_specs=out_specs, check_vma=False)
```

```python
import functools

import jax
import jax.numpy as jnp
from jax import lax
from jax.experimental import pallas as pl
from jax.experimental.pallas import tpu as pltpu
from jax.sharding import PartitionSpec as P

VG = 24
courant = 0.8
relax = 0.5
COLLISION_MAX = 0.0546875
TAIL = 16
LANES = 128
BF16 = jnp.bfloat16
F16 = jnp.float16
F32 = jnp.float32
HALF_MAX = 60000.0


def speeds(directions, offset, length):
    vel_index = offset + jnp.arange(length, dtype=jnp.int32)
    grid_x = vel_index // (VG * VG)
    grid_y = vel_index // VG % VG
    moving = 2 * directions - 1
    speed_x = courant * (grid_x.astype(F32) + 0.5) / VG
    speed_y = courant * (grid_y.astype(F32) - 0.5 * (VG - 1)) / VG
    return (moving, speed_x, speed_y)


def transverse(distribution, speed_y):
    width_y = distribution.shape[1]
    padded = jnp.pad(distribution, ((0, 0), (2, 2), (0, 0)))
    upward = speed_y > 0
    first_up = jnp.where(upward, padded[:, 1 : width_y + 1], padded[:, 3 : width_y + 3])
    second_up = jnp.where(upward, padded[:, 0:width_y], padded[:, 4 : width_y + 4])
    return jnp.abs(speed_y) * (1.5 * distribution - 2.0 * first_up + 0.5 * second_up)


def halo_pairs(size):
    up = [(i, i + 1) for i in range(size - 1)]
    down = [(j, i) for i, j in up]
    around = [(0, size - 1), (size - 1, 0)]
    return up, down, around


def advected(distribution, below, above, directions, wall_mask, offset):
    tile_len, _, local_vel = distribution.shape
    moving, speed_x, speed_y = speeds(directions, offset, local_vel)
    padded_x = jnp.concatenate([below, distribution, above], axis=0)
    first_up = jnp.where(moving > 0, padded_x[1 : tile_len + 1], padded_x[3 : tile_len + 3])
    second_up = jnp.where(moving > 0, padded_x[0:tile_len], padded_x[4 : tile_len + 4])
    adv_x = speed_x * (1.5 * distribution - 2.0 * first_up + 0.5 * second_up)
    adv_y = transverse(distribution, speed_y)
    open_cells = (1 - wall_mask).astype(F32)[:, :, None]
    return open_cells, open_cells * (distribution - adv_x - adv_y)


def pieces_kernel(place, f_ref, keep_ref, send_ref, turned, *, cells, piece):
    chip, core = place[0], place[1]
    length = cells * piece
    peak = jnp.zeros((LANES, LANES), F32)
    for start in range(0, length, LANES):
        block = f_ref[:, start : start + LANES]
        peak = jnp.maximum(peak, jnp.abs(block))
        turned[start : start + LANES, :] = block.T.astype(BF16)
    top = jnp.max(peak, axis=(0, 1), keepdims=True) * 1.02 + 1e-30
    tail = jnp.broadcast_to(top, (TAIL, LANES)).astype(BF16)
    for q in range(cells // 2):
        other = chip ^ q
        for out, side in ((keep_ref, core), (send_ref, 1 - core)):
            at = pl.multiple_of((2 * other + side) * piece, TAIL)
            out[q, :piece, :] = turned[pl.ds(at, piece), :]
            out[q, piece:, :] = tail


def split_pieces(distribution, place, cells):
    tile_len, width, local_vel = distribution.shape
    piece = local_vel // cells
    out = jax.ShapeDtypeStruct((cells // 2, piece + TAIL, LANES), BF16)
    return pl.pallas_call(
        functools.partial(pieces_kernel, cells=cells, piece=piece),
        out_shape=(out, out),
        in_specs=[pl.BlockSpec(memory_space=pltpu.SMEM), pl.BlockSpec(memory_space=pltpu.VMEM)],
        out_specs=(pl.BlockSpec(memory_space=pltpu.VMEM), pl.BlockSpec(memory_space=pltpu.VMEM)),
        scratch_shapes=[pltpu.VMEM((local_vel, LANES), BF16)],
        compiler_params=pltpu.CompilerParams(vmem_limit_bytes=10 << 20),
        cost_estimate=pl.CostEstimate(flops=local_vel * LANES, bytes_accessed=local_vel * LANES * 6, transcendentals=0),
        name="pieces",
    )(place, distribution.reshape(tile_len * width, local_vel))


def product_kernel(place, own, gx, gy, dx, dy, c_ref, keep_ref, send_ref, scale_ref, rows, lhs, *, piece, bound):
    slots = own.shape[0]

    @pl.when(place[2] >= 0)
    def _():
        for s in range(slots):
            for side in range(2):
                diagonal = dx if side == 0 else dy
                parts = ((0, own.at[s, side]), (1, gx.at[s, side]), (2, gy.at[s, side]), (3, diagonal.at[s]))
                top = jnp.zeros((TAIL, LANES), F32)
                for q, part in parts:
                    at = pl.multiple_of((place[2] ^ q) * piece, TAIL)
                    rows[2 * s + side, pl.ds(at, piece), :] = part[:piece, :]
                    top = jnp.maximum(top, part[piece:, :].astype(F32))
                scale_ref[s, side] = bound / top[:8, :]

    @pl.when(place[1] >= 0)
    def _():
        for k in range(2 * slots):
            lhs[k * LANES : (k + 1) * LANES, :] = rows[k].T

    for s in range(slots):
        out = jnp.dot(lhs[2 * s * LANES : 2 * (s + 1) * LANES, :], c_ref[...], preferred_element_type=F32)
        keep_ref[s] = out[:LANES] * scale_ref[s, 0, 0:1, 0:1]
        send_ref[s] = out[LANES:] * scale_ref[s, 1, 0:1, 0:1]


def product(place, own, gx, gy, dx, dy, matrix, vels):
    slots = own.shape[0]
    piece = own.shape[2] - TAIL
    depth, columns = matrix.shape
    out = jax.ShapeDtypeStruct((slots, LANES, columns), F32)
    vmem = pl.BlockSpec(memory_space=pltpu.VMEM)
    return pl.pallas_call(
        functools.partial(product_kernel, piece=piece, bound=HALF_MAX / (vels * columns * COLLISION_MAX)),
        out_shape=(out, out, jax.ShapeDtypeStruct((slots, 2, 8, LANES), F32)),
        in_specs=[pl.BlockSpec(memory_space=pltpu.SMEM)] + [vmem] * 6,
        out_specs=(vmem, vmem, vmem),
        scratch_shapes=[pltpu.VMEM((2 * slots, depth, LANES), BF16), pltpu.VMEM((slots * 2 * LANES, depth), BF16)],
        compiler_params=pltpu.CompilerParams(vmem_limit_bytes=8 << 20),
        cost_estimate=pl.CostEstimate(
            flops=2 * slots * 2 * LANES * depth * columns,
            bytes_accessed=depth * columns * 2 + slots * 2 * LANES * columns * 4,
            transcendentals=0,
        ),
        name="product",
    )(place, own, gx, gy, dx, dy, matrix)


def load_kernel(c_ref, out_ref, sem):
    copy = pltpu.make_async_copy(c_ref, out_ref, sem)
    copy.start()
    copy.wait()


def loaded(matrix):
    return pl.pallas_call(
        load_kernel,
        out_shape=jax.ShapeDtypeStruct(matrix.shape, matrix.dtype),
        in_specs=[pl.BlockSpec(memory_space=pltpu.HBM)],
        out_specs=pl.BlockSpec(memory_space=pltpu.VMEM),
        scratch_shapes=[pltpu.SemaphoreType.DMA],
        compiler_params=pltpu.CompilerParams(vmem_limit_bytes=1 << 20),
        cost_estimate=pl.CostEstimate(flops=1, bytes_accessed=2 * matrix.size * 2, transcendentals=0),
        name="load",
    )(matrix)


def edge_kernel(place, a_ref, c_ref, d_ref, out_ref, *, cells):
    chip, core = place[0], place[1]
    cell = 2 * chip + core
    last = cells // 2 - 1
    is_end = jnp.logical_or(chip == 0, chip == last)
    held = ((a_ref, jnp.where(is_end, 3, 0)), (c_ref, jnp.where(is_end, 1, 3)), (d_ref, jnp.where(is_end, 0, 1)))
    for k, other in enumerate(((cell + cells - 1) % cells, (cell + 1) % cells)):
        total = jnp.zeros((TAIL, LANES), F32)
        for ref, q in held:
            for side in range(2):
                here = jnp.logical_and((other // 2) ^ chip == q, (other % 2) ^ core == side)
                tail = ref[0, side, ref.shape[2] - TAIL :, :].astype(F32)
                total = total + jnp.where(here, tail, jnp.zeros_like(tail))
        out_ref[k] = total[:8] * (1.0 / HALF_MAX)


def edge_scales(place, a, c, d, cells):
    vmem = pl.BlockSpec(memory_space=pltpu.VMEM)
    return pl.pallas_call(
        functools.partial(edge_kernel, cells=cells),
        out_shape=jax.ShapeDtypeStruct((2, 8, LANES), F32),
        in_specs=[pl.BlockSpec(memory_space=pltpu.SMEM), vmem, vmem, vmem],
        out_specs=vmem,
        compiler_params=pltpu.CompilerParams(vmem_limit_bytes=4 << 20),
        cost_estimate=pl.CostEstimate(flops=10000, bytes_accessed=10000, transcendentals=0),
        name="edges",
    )(place, a, c, d)


def after(value, *earlier):
    return lax.optimization_barrier((value,) + earlier)[0]


def chain_body(distribution, collision, directions, wall_mask):
    tile_len, width, local_vel = distribution.shape
    cells = lax.axis_size("cell")
    cell = lax.axis_index("cell")
    vel = lax.axis_index("vel")
    place = jnp.stack([cell >> 1, cell & 1, vel])
    is_end = jnp.logical_or(cell < 2, cell >= cells - 2)
    distribution, place, is_end, offset = lax.optimization_barrier((distribution, place, is_end, vel * local_vel))
    matrix = collision.reshape(-1, local_vel)

    other_core = [(i, i ^ 1) for i in range(cells)]
    across = lambda q: [(i, 2 * ((i // 2) ^ q) + i % 2) for i in range(cells)]
    in_x = [(i, i ^ 1) for i in range(4)]
    in_y = [(i, i ^ 2) for i in range(4)]
    chips = lambda *pairs: [(2 * a + c, 2 * b + c) for a, b in pairs for c in range(2)]
    ends = chips((0, 1), (3, 2))
    middle = chips((1, 2), (2, 1))
    outward = chips((2, 3), (1, 0))
    ring = [(i, (i + 1) % cells) for i in range(cells)]

    def gather_x_y(own):
        return own, lax.ppermute(own, "vel", in_x), lax.ppermute(own, "vel", in_y)

    def gather_diagonal(parts, *earlier):
        own, gx, gy = parts
        dx = lax.ppermute(after(gx[:, 0], *earlier), "vel", in_y)
        dy = lax.ppermute(after(gy[:, 1], *earlier), "vel", in_x)
        return own, gx, gy, dx, dy

    def exchanged(mine, theirs):
        theirs = lax.ppermute(theirs.astype(F16), "cell", other_core)
        return [mine[s] + theirs[s].astype(F32) for s in range(mine.shape[0])]

    def behind(parts, *earlier):
        return (after(parts[0], *earlier),) + tuple(parts[1:])

    keep, send = split_pieces(distribution, place, cells)
    got = lax.ppermute(send, "cell", other_core)
    matrix = loaded(pltpu.with_memory_space_constraint(after(matrix, got), pltpu.HBM))
    both = [jnp.stack([keep[q], got[q]])[None] for q in range(4)]

    from_end = lax.ppermute(both[3], "cell", chips((0, 3), (3, 0)))
    both1, both2, both3, from_end, matrix = lax.optimization_barrier((both[1], both[2], both[3], from_end, matrix))
    ga = gather_x_y(jnp.where(is_end, from_end, both[0]))
    slot_a = ga[0]
    slot_b = lax.ppermute(both2, "cell", across(2))
    z1 = lax.ppermute(both1, "cell", across(1))
    from_middle = lax.ppermute(both3, "cell", middle)
    ga = gather_diagonal(ga)
    mine_a, theirs_a, scale_a = product(place, *ga, matrix, 4)
    theirs_a, slot_b, z1, from_middle = lax.optimization_barrier((theirs_a, slot_b, z1, from_middle))
    (pa,) = exchanged(mine_a, theirs_a)
    ma = pa.astype(F16)
    a0 = lax.ppermute(ma, "cell", ends)
    gb = gather_x_y(after(slot_b, ma))
    gb = gather_diagonal(gb, ma)
    mine_b, theirs_b, _ = product(place, *gb, matrix, 4)
    (pb,) = exchanged(mine_b, theirs_b)
    mb = pb.astype(F16)
    a1 = lax.ppermute(after(mb, a0), "cell", ends)
    b1 = lax.ppermute((pb + a0.astype(F32)).astype(F16), "cell", middle)
    own_top = keep[0:1, keep.shape[1] - 1 :, 0:1].astype(F32)
    edges = after(distribution, a0) * (HALF_MAX / own_top)
    from_below = lax.ppermute(edges[tile_len - 2 :].astype(F16), "cell", ring)
    from_above = lax.ppermute(edges[:2].astype(F16), "cell", [(j, i) for i, j in ring])
    z1, from_middle, both0, _ = lax.optimization_barrier((z1, from_middle, both[0], gb[1]))
    slot_c = jnp.where(is_end, z1, from_middle)
    slot_d = jnp.where(is_end, both0, z1)
    gcd = gather_x_y(jnp.concatenate([slot_c, slot_d]))
    gcd = gather_diagonal(gcd, mb)
    mine_cd, theirs_cd, scale_cd = product(place, *behind(gcd, mb), matrix, 4)
    theirs_cd, from_below, from_above = lax.optimization_barrier((theirs_cd, from_below, from_above))
    pc, pd = exchanged(mine_cd, theirs_cd)
    a2 = lax.ppermute(after(pc.astype(F16), a1), "cell", ends)
    b2 = lax.ppermute((pc + a1.astype(F32)).astype(F16), "cell", middle)
    c2 = lax.ppermute((pd + b1.astype(F32)).astype(F16), "cell", outward)

    edge = edge_scales(place, *lax.optimization_barrier((slot_a, slot_c, slot_d, mb))[:3], cells)
    below = from_below.astype(F32) * edge[0:1, :1, :1]
    above = from_above.astype(F32) * edge[1:2, :1, :1]
    open_cells, base = advected(after(distribution, mb), below, above, directions, wall_mask, offset)
    scale = jnp.where(is_end, scale_cd[1, 0:1, :1, :1], scale_a[0, 0:1, :1, :1])
    own = jnp.where(is_end, pd, pa)
    factor = open_cells * (relax / scale)
    base, factor, own = lax.optimization_barrier((base, factor, own))
    arrived = a2.astype(F32) + b2.astype(F32) + c2.astype(F32)
    return base + factor * (own + arrived).reshape(distribution.shape)


def plain_body(distribution, collision, directions, wall_mask):
    tile_len, width, local_vel = distribution.shape
    cells = lax.axis_size("cell")
    vels = lax.axis_size("vel")
    cell = lax.axis_index("cell")
    piece = local_vel // cells
    up, down, around = halo_pairs(cells)
    head, foot = distribution[:2], distribution[tile_len - 2 :]
    from_around = lax.ppermute(jnp.where(cell == 0, head, foot), "cell", around)
    below = jnp.where(cell == 0, from_around, lax.ppermute(foot, "cell", up))
    above = jnp.where(cell == cells - 1, from_around, lax.ppermute(head, "cell", down))
    offset = lax.axis_index("vel") * local_vel
    open_cells, base = advected(distribution, below, above, directions, wall_mask, offset)
    pieces = distribution.astype(BF16).reshape(tile_len * width, cells, piece)
    spread = lax.all_to_all(pieces, "cell", split_axis=1, concat_axis=0, tiled=True)
    panel = lax.all_gather(spread.reshape(-1, piece), "vel", axis=1, tiled=True)
    part = jnp.dot(panel, collision.reshape(vels * piece, local_vel), preferred_element_type=F32)
    gain = lax.psum_scatter(part, "cell", scatter_dimension=0, tiled=True)
    return base + open_cells * relax * gain.reshape(distribution.shape)


def body(distribution, collision, directions, wall_mask):
    tile_len, width, local_vel = distribution.shape
    cells = lax.axis_size("cell")
    piece = local_vel // cells
    fits = tile_len * width == LANES and piece % TAIL == 0 and local_vel % (3 * LANES) == 0
    if cells == 8 and lax.axis_size("vel") == 4 and fits:
        return chain_body(distribution, collision, directions, wall_mask)
    return plain_body(distribution, collision, directions, wall_mask)


def solution(mesh):
    in_specs = (P("cell", None, "vel"), P(None, "cell", None, "vel"), P("vel"), P("cell", None))
    out_specs = P("cell", None, "vel")
    return jax.shard_map(body, mesh=mesh, in_specs=in_specs, out_specs=out_specs, check_vma=False)
```

```python
import functools

import jax
import jax.numpy as jnp
from jax import lax
from jax.experimental import pallas as pl
from jax.experimental.pallas import tpu as pltpu
from jax.sharding import PartitionSpec as P

VG = 24
courant = 0.8
relax = 0.5
COLLISION_MAX = 0.0546875
TAIL = 16
LANES = 128
BF16 = jnp.bfloat16
F16 = jnp.float16
F32 = jnp.float32
HALF_MAX = 60000.0


def speeds(directions, offset, length):
    vel_index = offset + jnp.arange(length, dtype=jnp.int32)
    grid_x = vel_index // (VG * VG)
    grid_y = vel_index // VG % VG
    moving = 2 * directions - 1
    speed_x = courant * (grid_x.astype(F32) + 0.5) / VG
    speed_y = courant * (grid_y.astype(F32) - 0.5 * (VG - 1)) / VG
    return (moving, speed_x, speed_y)


def transverse(distribution, speed_y):
    width_y = distribution.shape[1]
    padded = jnp.pad(distribution, ((0, 0), (2, 2), (0, 0)))
    upward = speed_y > 0
    first_up = jnp.where(upward, padded[:, 1 : width_y + 1], padded[:, 3 : width_y + 3])
    second_up = jnp.where(upward, padded[:, 0:width_y], padded[:, 4 : width_y + 4])
    return jnp.abs(speed_y) * (1.5 * distribution - 2.0 * first_up + 0.5 * second_up)


def halo_pairs(size):
    up = [(i, i + 1) for i in range(size - 1)]
    down = [(j, i) for i, j in up]
    around = [(0, size - 1), (size - 1, 0)]
    return up, down, around


def advected(distribution, below, above, directions, wall_mask, offset):
    tile_len, _, local_vel = distribution.shape
    moving, speed_x, speed_y = speeds(directions, offset, local_vel)
    padded_x = jnp.concatenate([below, distribution, above], axis=0)
    first_up = jnp.where(moving > 0, padded_x[1 : tile_len + 1], padded_x[3 : tile_len + 3])
    second_up = jnp.where(moving > 0, padded_x[0:tile_len], padded_x[4 : tile_len + 4])
    adv_x = speed_x * (1.5 * distribution - 2.0 * first_up + 0.5 * second_up)
    adv_y = transverse(distribution, speed_y)
    open_cells = (1 - wall_mask).astype(F32)[:, :, None]
    return open_cells, open_cells * (distribution - adv_x - adv_y)


def pieces_kernel(place, f_ref, keep_ref, send_ref, turned, *, cells, piece):
    chip, core = place[0], place[1]
    length = cells * piece
    peak = jnp.zeros((LANES, LANES), F32)
    for start in range(0, length, LANES):
        block = f_ref[:, start : start + LANES]
        peak = jnp.maximum(peak, jnp.abs(block))
        turned[start : start + LANES, :] = block.T.astype(BF16)
    top = jnp.max(peak, axis=(0, 1), keepdims=True) * 1.02 + 1e-30
    tail = jnp.broadcast_to(top, (TAIL, LANES)).astype(BF16)
    for q in range(cells // 2):
        other = chip ^ q
        for out, side in ((keep_ref, core), (send_ref, 1 - core)):
            at = pl.multiple_of((2 * other + side) * piece, TAIL)
            out[q, :piece, :] = turned[pl.ds(at, piece), :]
            out[q, piece:, :] = tail


def split_pieces(distribution, place, cells):
    tile_len, width, local_vel = distribution.shape
    piece = local_vel // cells
    out = jax.ShapeDtypeStruct((cells // 2, piece + TAIL, LANES), BF16)
    return pl.pallas_call(
        functools.partial(pieces_kernel, cells=cells, piece=piece),
        out_shape=(out, out),
        in_specs=[pl.BlockSpec(memory_space=pltpu.SMEM), pl.BlockSpec(memory_space=pltpu.VMEM)],
        out_specs=(pl.BlockSpec(memory_space=pltpu.VMEM), pl.BlockSpec(memory_space=pltpu.VMEM)),
        scratch_shapes=[pltpu.VMEM((local_vel, LANES), BF16)],
        compiler_params=pltpu.CompilerParams(vmem_limit_bytes=10 << 20),
        cost_estimate=pl.CostEstimate(flops=local_vel * LANES, bytes_accessed=local_vel * LANES * 6, transcendentals=0),
        name="pieces",
    )(place, distribution.reshape(tile_len * width, local_vel))


def product_kernel(place, own, gx, gy, dx, dy, c_ref, keep_ref, send_ref, scale_ref, rows, lhs, *, piece, bound):
    slots = own.shape[0]

    @pl.when(place[2] >= 0)
    def _():
        for s in range(slots):
            for side in range(2):
                diagonal = dx if side == 0 else dy
                parts = ((0, own.at[s, side]), (1, gx.at[s, side]), (2, gy.at[s, side]), (3, diagonal.at[s]))
                top = jnp.zeros((TAIL, LANES), F32)
                for q, part in parts:
                    at = pl.multiple_of((place[2] ^ q) * piece, TAIL)
                    rows[2 * s + side, pl.ds(at, piece), :] = part[:piece, :]
                    top = jnp.maximum(top, part[piece:, :].astype(F32))
                scale_ref[s, side] = bound / top[:8, :]

    @pl.when(place[1] >= 0)
    def _():
        for k in range(2 * slots):
            lhs[k * LANES : (k + 1) * LANES, :] = rows[k].T

    for s in range(slots):
        out = jnp.dot(lhs[2 * s * LANES : 2 * (s + 1) * LANES, :], c_ref[...], preferred_element_type=F32)
        keep_ref[s] = out[:LANES] * scale_ref[s, 0, 0:1, 0:1]
        send_ref[s] = out[LANES:] * scale_ref[s, 1, 0:1, 0:1]


def product(place, own, gx, gy, dx, dy, matrix, vels):
    slots = own.shape[0]
    piece = own.shape[2] - TAIL
    depth, columns = matrix.shape
    out = jax.ShapeDtypeStruct((slots, LANES, columns), F32)
    vmem = pl.BlockSpec(memory_space=pltpu.VMEM)
    return pl.pallas_call(
        functools.partial(product_kernel, piece=piece, bound=HALF_MAX / (vels * columns * COLLISION_MAX)),
        out_shape=(out, out, jax.ShapeDtypeStruct((slots, 2, 8, LANES), F32)),
        in_specs=[pl.BlockSpec(memory_space=pltpu.SMEM)] + [vmem] * 6,
        out_specs=(vmem, vmem, vmem),
        scratch_shapes=[pltpu.VMEM((2 * slots, depth, LANES), BF16), pltpu.VMEM((slots * 2 * LANES, depth), BF16)],
        compiler_params=pltpu.CompilerParams(vmem_limit_bytes=8 << 20),
        cost_estimate=pl.CostEstimate(
            flops=2 * slots * 2 * LANES * depth * columns,
            bytes_accessed=depth * columns * 2 + slots * 2 * LANES * columns * 4,
            transcendentals=0,
        ),
        name="product",
    )(place, own, gx, gy, dx, dy, matrix)


def load_kernel(c_ref, out_ref, sem):
    copy = pltpu.make_async_copy(c_ref, out_ref, sem)
    copy.start()
    copy.wait()


def loaded(matrix):
    return pl.pallas_call(
        load_kernel,
        out_shape=jax.ShapeDtypeStruct(matrix.shape, matrix.dtype),
        in_specs=[pl.BlockSpec(memory_space=pltpu.HBM)],
        out_specs=pl.BlockSpec(memory_space=pltpu.VMEM),
        scratch_shapes=[pltpu.SemaphoreType.DMA],
        compiler_params=pltpu.CompilerParams(vmem_limit_bytes=1 << 20),
        cost_estimate=pl.CostEstimate(flops=1, bytes_accessed=2 * matrix.size * 2, transcendentals=0),
        name="load",
    )(matrix)


def edge_kernel(place, a_ref, c_ref, d_ref, out_ref, *, cells):
    chip, core = place[0], place[1]
    cell = 2 * chip + core
    last = cells // 2 - 1
    is_end = jnp.logical_or(chip == 0, chip == last)
    held = ((a_ref, jnp.where(is_end, 3, 0)), (c_ref, jnp.where(is_end, 1, 3)), (d_ref, jnp.where(is_end, 0, 1)))
    for k, other in enumerate(((cell + cells - 1) % cells, (cell + 1) % cells)):
        total = jnp.zeros((TAIL, LANES), F32)
        for ref, q in held:
            for side in range(2):
                here = jnp.logical_and((other // 2) ^ chip == q, (other % 2) ^ core == side)
                tail = ref[0, side, ref.shape[2] - TAIL :, :].astype(F32)
                total = total + jnp.where(here, tail, jnp.zeros_like(tail))
        out_ref[k] = total[:8] * (1.0 / HALF_MAX)


def edge_scales(place, a, c, d, cells):
    vmem = pl.BlockSpec(memory_space=pltpu.VMEM)
    return pl.pallas_call(
        functools.partial(edge_kernel, cells=cells),
        out_shape=jax.ShapeDtypeStruct((2, 8, LANES), F32),
        in_specs=[pl.BlockSpec(memory_space=pltpu.SMEM), vmem, vmem, vmem],
        out_specs=vmem,
        compiler_params=pltpu.CompilerParams(vmem_limit_bytes=4 << 20),
        cost_estimate=pl.CostEstimate(flops=10000, bytes_accessed=10000, transcendentals=0),
        name="edges",
    )(place, a, c, d)


def after(value, *earlier):
    return lax.optimization_barrier((value,) + earlier)[0]


def chain_body(distribution, collision, directions, wall_mask):
    tile_len, width, local_vel = distribution.shape
    cells = lax.axis_size("cell")
    cell = lax.axis_index("cell")
    vel = lax.axis_index("vel")
    place = jnp.stack([cell >> 1, cell & 1, vel])
    is_end = jnp.logical_or(cell < 2, cell >= cells - 2)
    distribution, place, is_end, offset = lax.optimization_barrier((distribution, place, is_end, vel * local_vel))
    matrix = collision.reshape(-1, local_vel)

    other_core = [(i, i ^ 1) for i in range(cells)]
    across = lambda q: [(i, 2 * ((i // 2) ^ q) + i % 2) for i in range(cells)]
    in_x = [(i, i ^ 1) for i in range(4)]
    in_y = [(i, i ^ 2) for i in range(4)]
    chips = lambda *pairs: [(2 * a + c, 2 * b + c) for a, b in pairs for c in range(2)]
    ends = chips((0, 1), (3, 2))
    middle = chips((1, 2), (2, 1))
    outward = chips((2, 3), (1, 0))
    ring = [(i, (i + 1) % cells) for i in range(cells)]

    def gather_x_y(own):
        return own, lax.ppermute(own, "vel", in_x), lax.ppermute(own, "vel", in_y)

    def gather_diagonal(parts, *earlier):
        own, gx, gy = parts
        dx = lax.ppermute(after(gx[:, 0], *earlier), "vel", in_y)
        dy = lax.ppermute(after(gy[:, 1], *earlier), "vel", in_x)
        return own, gx, gy, dx, dy

    def exchanged(mine, theirs):
        theirs = lax.ppermute(theirs.astype(F16), "cell", other_core)
        return [mine[s] + theirs[s].astype(F32) for s in range(mine.shape[0])]

    def behind(parts, *earlier):
        return (after(parts[0], *earlier),) + tuple(parts[1:])

    keep, send = split_pieces(distribution, place, cells)
    got = lax.ppermute(send, "cell", other_core)
    matrix = loaded(pltpu.with_memory_space_constraint(after(matrix, got), pltpu.HBM))
    both = [jnp.stack([keep[q], got[q]])[None] for q in range(4)]

    z3 = lax.ppermute(both[3], "cell", across(3))
    both1, both2, z3, matrix = lax.optimization_barrier((both[1], both[2], z3, matrix))
    ga = gather_x_y(jnp.where(is_end, z3, both[0]))
    slot_a = ga[0]
    slot_b = lax.ppermute(both2, "cell", across(2))
    z1 = lax.ppermute(both1, "cell", across(1))
    ga = gather_diagonal(ga)
    mine_a, theirs_a, scale_a = product(place, *ga, matrix, 4)
    theirs_a, slot_b, z1 = lax.optimization_barrier((theirs_a, slot_b, z1))
    (pa,) = exchanged(mine_a, theirs_a)
    ma = pa.astype(F16)
    a0 = lax.ppermute(ma, "cell", ends)
    gb = gather_x_y(after(slot_b, ma))
    gb = gather_diagonal(gb, ma)
    mine_b, theirs_b, _ = product(place, *gb, matrix, 4)
    (pb,) = exchanged(mine_b, theirs_b)
    mb = pb.astype(F16)
    a1 = lax.ppermute(after(mb, a0), "cell", ends)
    b1 = lax.ppermute((pb + a0.astype(F32)).astype(F16), "cell", middle)
    own_top = keep[0:1, keep.shape[1] - 1 :, 0:1].astype(F32)
    edges = after(distribution, a0) * (HALF_MAX / own_top)
    from_below = lax.ppermute(edges[tile_len - 2 :].astype(F16), "cell", ring)
    from_above = lax.ppermute(edges[:2].astype(F16), "cell", [(j, i) for i, j in ring])
    z1, z3, both0, _ = lax.optimization_barrier((z1, z3, both[0], gb[1]))
    slot_c = jnp.where(is_end, z1, z3)
    slot_d = jnp.where(is_end, both0, z1)
    gcd = gather_x_y(jnp.concatenate([slot_c, slot_d]))
    gcd = gather_diagonal(gcd, mb)
    mine_cd, theirs_cd, scale_cd = product(place, *behind(gcd, mb), matrix, 4)
    theirs_cd, from_below, from_above = lax.optimization_barrier((theirs_cd, from_below, from_above))
    pc, pd = exchanged(mine_cd, theirs_cd)
    mc2 = (pd + b1.astype(F32)).astype(F16)
    c2 = lax.ppermute(mc2, "cell", outward)
    a2 = lax.ppermute(after(pc.astype(F16), a1, mc2), "cell", ends)
    b2 = lax.ppermute((pc + a1.astype(F32)).astype(F16), "cell", middle)

    edge = edge_scales(place, *lax.optimization_barrier((slot_a, slot_c, slot_d, mb))[:3], cells)
    below = from_below.astype(F32) * edge[0:1, :1, :1]
    above = from_above.astype(F32) * edge[1:2, :1, :1]
    open_cells, base = advected(after(distribution, mb), below, above, directions, wall_mask, offset)
    scale = jnp.where(is_end, scale_cd[1, 0:1, :1, :1], scale_a[0, 0:1, :1, :1])
    own = jnp.where(is_end, pd, pa)
    factor = open_cells * (relax / scale)
    base, factor, own = lax.optimization_barrier((base, factor, own))
    arrived = a2.astype(F32) + b2.astype(F32) + c2.astype(F32)
    return base + factor * (own + arrived).reshape(distribution.shape)


def plain_body(distribution, collision, directions, wall_mask):
    tile_len, width, local_vel = distribution.shape
    cells = lax.axis_size("cell")
    vels = lax.axis_size("vel")
    cell = lax.axis_index("cell")
    piece = local_vel // cells
    up, down, around = halo_pairs(cells)
    head, foot = distribution[:2], distribution[tile_len - 2 :]
    from_around = lax.ppermute(jnp.where(cell == 0, head, foot), "cell", around)
    below = jnp.where(cell == 0, from_around, lax.ppermute(foot, "cell", up))
    above = jnp.where(cell == cells - 1, from_around, lax.ppermute(head, "cell", down))
    offset = lax.axis_index("vel") * local_vel
    open_cells, base = advected(distribution, below, above, directions, wall_mask, offset)
    pieces = distribution.astype(BF16).reshape(tile_len * width, cells, piece)
    spread = lax.all_to_all(pieces, "cell", split_axis=1, concat_axis=0, tiled=True)
    panel = lax.all_gather(spread.reshape(-1, piece), "vel", axis=1, tiled=True)
    part = jnp.dot(panel, collision.reshape(vels * piece, local_vel), preferred_element_type=F32)
    gain = lax.psum_scatter(part, "cell", scatter_dimension=0, tiled=True)
    return base + open_cells * relax * gain.reshape(distribution.shape)


def body(distribution, collision, directions, wall_mask):
    tile_len, width, local_vel = distribution.shape
    cells = lax.axis_size("cell")
    piece = local_vel // cells
    fits = tile_len * width == LANES and piece % TAIL == 0 and local_vel % (3 * LANES) == 0
    if cells == 8 and lax.axis_size("vel") == 4 and fits:
        return chain_body(distribution, collision, directions, wall_mask)
    return plain_body(distribution, collision, directions, wall_mask)


def solution(mesh):
    in_specs = (P("cell", None, "vel"), P(None, "cell", None, "vel"), P("vel"), P("cell", None))
    out_specs = P("cell", None, "vel")
    return jax.shard_map(body, mesh=mesh, in_specs=in_specs, out_specs=out_specs, check_vma=False)
```

```python
import functools

import jax
import jax.numpy as jnp
from jax import lax
from jax.experimental import pallas as pl
from jax.experimental.pallas import tpu as pltpu
from jax.sharding import PartitionSpec as P

VG = 24
courant = 0.8
relax = 0.5
COLLISION_MAX = 0.0546875
TAIL = 16
LANES = 128
BF16 = jnp.bfloat16
F16 = jnp.float16
F32 = jnp.float32
HALF_MAX = 60000.0


def speeds(directions, offset, length):
    vel_index = offset + jnp.arange(length, dtype=jnp.int32)
    grid_x = vel_index // (VG * VG)
    grid_y = vel_index // VG % VG
    moving = 2 * directions - 1
    speed_x = courant * (grid_x.astype(F32) + 0.5) / VG
    speed_y = courant * (grid_y.astype(F32) - 0.5 * (VG - 1)) / VG
    return (moving, speed_x, speed_y)


def transverse(distribution, speed_y):
    width_y = distribution.shape[1]
    padded = jnp.pad(distribution, ((0, 0), (2, 2), (0, 0)))
    upward = speed_y > 0
    first_up = jnp.where(upward, padded[:, 1 : width_y + 1], padded[:, 3 : width_y + 3])
    second_up = jnp.where(upward, padded[:, 0:width_y], padded[:, 4 : width_y + 4])
    return jnp.abs(speed_y) * (1.5 * distribution - 2.0 * first_up + 0.5 * second_up)


def halo_pairs(size):
    up = [(i, i + 1) for i in range(size - 1)]
    down = [(j, i) for i, j in up]
    around = [(0, size - 1), (size - 1, 0)]
    return up, down, around


def advected(distribution, below, above, directions, wall_mask, offset):
    tile_len, _, local_vel = distribution.shape
    moving, speed_x, speed_y = speeds(directions, offset, local_vel)
    padded_x = jnp.concatenate([below, distribution, above], axis=0)
    first_up = jnp.where(moving > 0, padded_x[1 : tile_len + 1], padded_x[3 : tile_len + 3])
    second_up = jnp.where(moving > 0, padded_x[0:tile_len], padded_x[4 : tile_len + 4])
    adv_x = speed_x * (1.5 * distribution - 2.0 * first_up + 0.5 * second_up)
    adv_y = transverse(distribution, speed_y)
    open_cells = (1 - wall_mask).astype(F32)[:, :, None]
    return open_cells, open_cells * (distribution - adv_x - adv_y)


def pieces_kernel(place, f_ref, keep_ref, send_ref, turned, *, cells, piece):
    chip, core = place[0], place[1]
    length = cells * piece
    peak = jnp.zeros((LANES, LANES), F32)
    for start in range(0, length, LANES):
        block = f_ref[:, start : start + LANES]
        peak = jnp.maximum(peak, jnp.abs(block))
        turned[start : start + LANES, :] = block.T.astype(BF16)
    top = jnp.max(peak, axis=(0, 1), keepdims=True) * 1.02 + 1e-30
    tail = jnp.broadcast_to(top, (TAIL, LANES)).astype(BF16)
    for q in range(cells // 2):
        other = chip ^ q
        for out, side in ((keep_ref, core), (send_ref, 1 - core)):
            at = pl.multiple_of((2 * other + side) * piece, TAIL)
            out[q, :piece, :] = turned[pl.ds(at, piece), :]
            out[q, piece:, :] = tail


def split_pieces(distribution, place, cells):
    tile_len, width, local_vel = distribution.shape
    piece = local_vel // cells
    out = jax.ShapeDtypeStruct((cells // 2, piece + TAIL, LANES), BF16)
    return pl.pallas_call(
        functools.partial(pieces_kernel, cells=cells, piece=piece),
        out_shape=(out, out),
        in_specs=[pl.BlockSpec(memory_space=pltpu.SMEM), pl.BlockSpec(memory_space=pltpu.VMEM)],
        out_specs=(pl.BlockSpec(memory_space=pltpu.VMEM), pl.BlockSpec(memory_space=pltpu.VMEM)),
        scratch_shapes=[pltpu.VMEM((local_vel, LANES), BF16)],
        compiler_params=pltpu.CompilerParams(vmem_limit_bytes=10 << 20),
        cost_estimate=pl.CostEstimate(flops=local_vel * LANES, bytes_accessed=local_vel * LANES * 6, transcendentals=0),
        name="pieces",
    )(place, distribution.reshape(tile_len * width, local_vel))


def product_kernel(place, own, gx, gy, dx, dy, c_ref, keep_ref, send_ref, scale_ref, rows, lhs, *, piece, bound):
    slots = own.shape[0]

    @pl.when(place[2] >= 0)
    def _():
        for s in range(slots):
            for side in range(2):
                diagonal = dx if side == 0 else dy
                parts = ((0, own.at[s, side]), (1, gx.at[s, side]), (2, gy.at[s, side]), (3, diagonal.at[s]))
                top = jnp.zeros((TAIL, LANES), F32)
                for q, part in parts:
                    at = pl.multiple_of((place[2] ^ q) * piece, TAIL)
                    rows[2 * s + side, pl.ds(at, piece), :] = part[:piece, :]
                    top = jnp.maximum(top, part[piece:, :].astype(F32))
                scale_ref[s, side] = bound / top[:8, :]

    @pl.when(place[1] >= 0)
    def _():
        for k in range(2 * slots):
            lhs[k * LANES : (k + 1) * LANES, :] = rows[k].T

    for s in range(slots):
        out = jnp.dot(lhs[2 * s * LANES : 2 * (s + 1) * LANES, :], c_ref[...], preferred_element_type=F32)
        keep_ref[s] = out[:LANES] * scale_ref[s, 0, 0:1, 0:1]
        send_ref[s] = out[LANES:] * scale_ref[s, 1, 0:1, 0:1]


def product(place, own, gx, gy, dx, dy, matrix, vels):
    slots = own.shape[0]
    piece = own.shape[2] - TAIL
    depth, columns = matrix.shape
    out = jax.ShapeDtypeStruct((slots, LANES, columns), F32)
    vmem = pl.BlockSpec(memory_space=pltpu.VMEM)
    return pl.pallas_call(
        functools.partial(product_kernel, piece=piece, bound=HALF_MAX / (vels * columns * COLLISION_MAX)),
        out_shape=(out, out, jax.ShapeDtypeStruct((slots, 2, 8, LANES), F32)),
        in_specs=[pl.BlockSpec(memory_space=pltpu.SMEM)] + [vmem] * 6,
        out_specs=(vmem, vmem, vmem),
        scratch_shapes=[pltpu.VMEM((2 * slots, depth, LANES), BF16), pltpu.VMEM((slots * 2 * LANES, depth), BF16)],
        compiler_params=pltpu.CompilerParams(vmem_limit_bytes=8 << 20),
        cost_estimate=pl.CostEstimate(
            flops=2 * slots * 2 * LANES * depth * columns,
            bytes_accessed=depth * columns * 2 + slots * 2 * LANES * columns * 4,
            transcendentals=0,
        ),
        name="product",
    )(place, own, gx, gy, dx, dy, matrix)


def load_kernel(c_ref, out_ref, sem):
    copy = pltpu.make_async_copy(c_ref, out_ref, sem)
    copy.start()
    copy.wait()


def loaded(matrix):
    return pl.pallas_call(
        load_kernel,
        out_shape=jax.ShapeDtypeStruct(matrix.shape, matrix.dtype),
        in_specs=[pl.BlockSpec(memory_space=pltpu.HBM)],
        out_specs=pl.BlockSpec(memory_space=pltpu.VMEM),
        scratch_shapes=[pltpu.SemaphoreType.DMA],
        compiler_params=pltpu.CompilerParams(vmem_limit_bytes=1 << 20),
        cost_estimate=pl.CostEstimate(flops=1, bytes_accessed=2 * matrix.size * 2, transcendentals=0),
        name="load",
    )(matrix)


def edge_kernel(place, a_ref, c_ref, d_ref, out_ref, *, cells):
    chip, core = place[0], place[1]
    cell = 2 * chip + core
    last = cells // 2 - 1
    is_end = jnp.logical_or(chip == 0, chip == last)
    held = ((a_ref, jnp.where(is_end, 3, 0)), (c_ref, jnp.where(is_end, 1, 3)), (d_ref, jnp.where(is_end, 0, 1)))
    for k, other in enumerate(((cell + cells - 1) % cells, (cell + 1) % cells)):
        total = jnp.zeros((TAIL, LANES), F32)
        for ref, q in held:
            for side in range(2):
                here = jnp.logical_and((other // 2) ^ chip == q, (other % 2) ^ core == side)
                tail = ref[0, side, ref.shape[2] - TAIL :, :].astype(F32)
                total = total + jnp.where(here, tail, jnp.zeros_like(tail))
        out_ref[k] = total[:8] * (1.0 / HALF_MAX)


def edge_scales(place, a, c, d, cells):
    vmem = pl.BlockSpec(memory_space=pltpu.VMEM)
    return pl.pallas_call(
        functools.partial(edge_kernel, cells=cells),
        out_shape=jax.ShapeDtypeStruct((2, 8, LANES), F32),
        in_specs=[pl.BlockSpec(memory_space=pltpu.SMEM), vmem, vmem, vmem],
        out_specs=vmem,
        compiler_params=pltpu.CompilerParams(vmem_limit_bytes=4 << 20),
        cost_estimate=pl.CostEstimate(flops=10000, bytes_accessed=10000, transcendentals=0),
        name="edges",
    )(place, a, c, d)


def after(value, *earlier):
    return lax.optimization_barrier((value,) + earlier)[0]


def chain_body(distribution, collision, directions, wall_mask):
    tile_len, width, local_vel = distribution.shape
    cells = lax.axis_size("cell")
    cell = lax.axis_index("cell")
    vel = lax.axis_index("vel")
    place = jnp.stack([cell >> 1, cell & 1, vel])
    is_end = jnp.logical_or(cell < 2, cell >= cells - 2)
    distribution, place, is_end, offset = lax.optimization_barrier((distribution, place, is_end, vel * local_vel))
    matrix = collision.reshape(-1, local_vel)

    other_core = [(i, i ^ 1) for i in range(cells)]
    across = lambda q: [(i, 2 * ((i // 2) ^ q) + i % 2) for i in range(cells)]
    in_x = [(i, i ^ 1) for i in range(4)]
    in_y = [(i, i ^ 2) for i in range(4)]
    chips = lambda *pairs: [(2 * a + c, 2 * b + c) for a, b in pairs for c in range(2)]
    ends = chips((0, 1), (3, 2))
    middle = chips((1, 2), (2, 1))
    outward = chips((2, 3), (1, 0))
    ring = [(i, (i + 1) % cells) for i in range(cells)]

    def gather_x_y(own):
        return own, lax.ppermute(own, "vel", in_x), lax.ppermute(own, "vel", in_y)

    def gather_diagonal(parts, *earlier):
        own, gx, gy = parts
        dx = lax.ppermute(after(gx[:, 0], *earlier), "vel", in_y)
        dy = lax.ppermute(after(gy[:, 1], *earlier), "vel", in_x)
        return own, gx, gy, dx, dy

    def exchanged(mine, theirs):
        theirs = lax.ppermute(theirs.astype(F16), "cell", other_core)
        return [mine[s] + theirs[s].astype(F32) for s in range(mine.shape[0])]

    def behind(parts, *earlier):
        return (after(parts[0], *earlier),) + tuple(parts[1:])

    keep, send = split_pieces(distribution, place, cells)
    got = lax.ppermute(send, "cell", other_core)
    matrix = loaded(pltpu.with_memory_space_constraint(after(matrix, got), pltpu.HBM))
    both = [jnp.stack([keep[q], got[q]])[None] for q in range(4)]

    z3 = lax.ppermute(both[3], "cell", across(3))
    both1, both2, z3, matrix = lax.optimization_barrier((both[1], both[2], z3, matrix))
    ga = gather_x_y(jnp.where(is_end, z3, both[0]))
    slot_a = ga[0]
    slot_b = lax.ppermute(both2, "cell", across(2))
    z1 = lax.ppermute(both1, "cell", across(1))
    ga = gather_diagonal(ga)
    mine_a, theirs_a, scale_a = product(place, *ga, matrix, 4)
    theirs_a, slot_b, z1 = lax.optimization_barrier((theirs_a, slot_b, z1))
    (pa,) = exchanged(mine_a, theirs_a)
    ma = pa.astype(F16)
    a0 = lax.ppermute(ma, "cell", ends)
    gb = gather_x_y(after(slot_b, ma))
    gb = gather_diagonal(gb, ma)
    mine_b, theirs_b, _ = product(place, *gb, matrix, 4)
    (pb,) = exchanged(mine_b, theirs_b)
    mb = pb.astype(F16)
    mb1 = (pb + a0.astype(F32)).astype(F16)
    b1 = lax.ppermute(mb1, "cell", middle)
    a1 = lax.ppermute(after(mb, a0, mb1), "cell", ends)
    own_top = keep[0:1, keep.shape[1] - 1 :, 0:1].astype(F32)
    edges = after(distribution, a0) * (HALF_MAX / own_top)
    from_below = lax.ppermute(edges[tile_len - 2 :].astype(F16), "cell", ring)
    from_above = lax.ppermute(edges[:2].astype(F16), "cell", [(j, i) for i, j in ring])
    z1, z3, both0, _ = lax.optimization_barrier((z1, z3, both[0], gb[2]))
    slot_c = jnp.where(is_end, z1, z3)
    slot_d = jnp.where(is_end, both0, z1)
    gcd = gather_x_y(jnp.concatenate([slot_c, slot_d]))
    gcd = gather_diagonal(gcd, mb)
    mine_cd, theirs_cd, scale_cd = product(place, *behind(gcd, mb), matrix, 4)
    theirs_cd, from_below, from_above = lax.optimization_barrier((theirs_cd, from_below, from_above))
    pc, pd = exchanged(mine_cd, theirs_cd)
    mc2 = (pd + b1.astype(F32)).astype(F16)
    c2 = lax.ppermute(mc2, "cell", outward)
    a2 = lax.ppermute(after(pc.astype(F16), a1, mc2), "cell", ends)
    b2 = lax.ppermute((pc + a1.astype(F32)).astype(F16), "cell", middle)

    edge = edge_scales(place, *lax.optimization_barrier((slot_a, slot_c, slot_d, mb))[:3], cells)
    below = from_below.astype(F32) * edge[0:1, :1, :1]
    above = from_above.astype(F32) * edge[1:2, :1, :1]
    open_cells, base = advected(after(distribution, mb), below, above, directions, wall_mask, offset)
    scale = jnp.where(is_end, scale_cd[1, 0:1, :1, :1], scale_a[0, 0:1, :1, :1])
    own = jnp.where(is_end, pd, pa)
    factor = open_cells * (relax / scale)
    base, factor, own = lax.optimization_barrier((base, factor, own))
    arrived = a2.astype(F32) + b2.astype(F32) + c2.astype(F32)
    return base + factor * (own + arrived).reshape(distribution.shape)


def plain_body(distribution, collision, directions, wall_mask):
    tile_len, width, local_vel = distribution.shape
    cells = lax.axis_size("cell")
    vels = lax.axis_size("vel")
    cell = lax.axis_index("cell")
    piece = local_vel // cells
    up, down, around = halo_pairs(cells)
    head, foot = distribution[:2], distribution[tile_len - 2 :]
    from_around = lax.ppermute(jnp.where(cell == 0, head, foot), "cell", around)
    below = jnp.where(cell == 0, from_around, lax.ppermute(foot, "cell", up))
    above = jnp.where(cell == cells - 1, from_around, lax.ppermute(head, "cell", down))
    offset = lax.axis_index("vel") * local_vel
    open_cells, base = advected(distribution, below, above, directions, wall_mask, offset)
    pieces = distribution.astype(BF16).reshape(tile_len * width, cells, piece)
    spread = lax.all_to_all(pieces, "cell", split_axis=1, concat_axis=0, tiled=True)
    panel = lax.all_gather(spread.reshape(-1, piece), "vel", axis=1, tiled=True)
    part = jnp.dot(panel, collision.reshape(vels * piece, local_vel), preferred_element_type=F32)
    gain = lax.psum_scatter(part, "cell", scatter_dimension=0, tiled=True)
    return base + open_cells * relax * gain.reshape(distribution.shape)


def body(distribution, collision, directions, wall_mask):
    tile_len, width, local_vel = distribution.shape
    cells = lax.axis_size("cell")
    piece = local_vel // cells
    fits = tile_len * width == LANES and piece % TAIL == 0 and local_vel % (3 * LANES) == 0
    if cells == 8 and lax.axis_size("vel") == 4 and fits:
        return chain_body(distribution, collision, directions, wall_mask)
    return plain_body(distribution, collision, directions, wall_mask)


def solution(mesh):
    in_specs = (P("cell", None, "vel"), P(None, "cell", None, "vel"), P("vel"), P("cell", None))
    out_specs = P("cell", None, "vel")
    return jax.shard_map(body, mesh=mesh, in_specs=in_specs, out_specs=out_specs, check_vma=False)
```

```python
import functools

import jax
import jax.numpy as jnp
from jax import lax
from jax.experimental import pallas as pl
from jax.experimental.pallas import tpu as pltpu
from jax.sharding import PartitionSpec as P

VG = 24
courant = 0.8
relax = 0.5
COLLISION_MAX = 0.0546875
TAIL = 16
LANES = 128
BF16 = jnp.bfloat16
F16 = jnp.float16
F32 = jnp.float32
HALF_MAX = 60000.0


def speeds(directions, offset, length):
    vel_index = offset + jnp.arange(length, dtype=jnp.int32)
    grid_x = vel_index // (VG * VG)
    grid_y = vel_index // VG % VG
    moving = 2 * directions - 1
    speed_x = courant * (grid_x.astype(F32) + 0.5) / VG
    speed_y = courant * (grid_y.astype(F32) - 0.5 * (VG - 1)) / VG
    return (moving, speed_x, speed_y)


def transverse(distribution, speed_y):
    width_y = distribution.shape[1]
    padded = jnp.pad(distribution, ((0, 0), (2, 2), (0, 0)))
    upward = speed_y > 0
    first_up = jnp.where(upward, padded[:, 1 : width_y + 1], padded[:, 3 : width_y + 3])
    second_up = jnp.where(upward, padded[:, 0:width_y], padded[:, 4 : width_y + 4])
    return jnp.abs(speed_y) * (1.5 * distribution - 2.0 * first_up + 0.5 * second_up)


def halo_pairs(size):
    up = [(i, i + 1) for i in range(size - 1)]
    down = [(j, i) for i, j in up]
    around = [(0, size - 1), (size - 1, 0)]
    return up, down, around


def advected(distribution, below, above, directions, wall_mask, offset):
    tile_len, _, local_vel = distribution.shape
    moving, speed_x, speed_y = speeds(directions, offset, local_vel)
    padded_x = jnp.concatenate([below, distribution, above], axis=0)
    first_up = jnp.where(moving > 0, padded_x[1 : tile_len + 1], padded_x[3 : tile_len + 3])
    second_up = jnp.where(moving > 0, padded_x[0:tile_len], padded_x[4 : tile_len + 4])
    adv_x = speed_x * (1.5 * distribution - 2.0 * first_up + 0.5 * second_up)
    adv_y = transverse(distribution, speed_y)
    open_cells = (1 - wall_mask).astype(F32)[:, :, None]
    return open_cells, open_cells * (distribution - adv_x - adv_y)


def pieces_kernel(place, f_ref, keep_ref, send_ref, turned, *, cells, piece):
    chip, core = place[0], place[1]
    length = cells * piece
    peak = jnp.zeros((LANES, LANES), F32)
    for start in range(0, length, LANES):
        block = f_ref[:, start : start + LANES]
        peak = jnp.maximum(peak, jnp.abs(block))
        turned[start : start + LANES, :] = block.T.astype(BF16)
    top = jnp.max(peak, axis=(0, 1), keepdims=True) * 1.02 + 1e-30
    tail = jnp.broadcast_to(top, (TAIL, LANES)).astype(BF16)
    for q in range(cells // 2):
        other = chip ^ q
        for out, side in ((keep_ref, core), (send_ref, 1 - core)):
            at = pl.multiple_of((2 * other + side) * piece, TAIL)
            out[q, :piece, :] = turned[pl.ds(at, piece), :]
            out[q, piece:, :] = tail


def split_pieces(distribution, place, cells):
    tile_len, width, local_vel = distribution.shape
    piece = local_vel // cells
    out = jax.ShapeDtypeStruct((cells // 2, piece + TAIL, LANES), BF16)
    return pl.pallas_call(
        functools.partial(pieces_kernel, cells=cells, piece=piece),
        out_shape=(out, out),
        in_specs=[pl.BlockSpec(memory_space=pltpu.SMEM), pl.BlockSpec(memory_space=pltpu.VMEM)],
        out_specs=(pl.BlockSpec(memory_space=pltpu.VMEM), pl.BlockSpec(memory_space=pltpu.VMEM)),
        scratch_shapes=[pltpu.VMEM((local_vel, LANES), BF16)],
        compiler_params=pltpu.CompilerParams(vmem_limit_bytes=10 << 20),
        cost_estimate=pl.CostEstimate(flops=local_vel * LANES, bytes_accessed=local_vel * LANES * 6, transcendentals=0),
        name="pieces",
    )(place, distribution.reshape(tile_len * width, local_vel))


def product_kernel(place, own, gx, gy, dx, dy, c_ref, keep_ref, send_ref, scale_ref, rows, lhs, *, piece, bound):
    slots = own.shape[0]

    @pl.when(place[2] >= 0)
    def _():
        for s in range(slots):
            for side in range(2):
                diagonal = dx if side == 0 else dy
                parts = ((0, own.at[s, side]), (1, gx.at[s, side]), (2, gy.at[s, side]), (3, diagonal.at[s]))
                top = jnp.zeros((TAIL, LANES), F32)
                for q, part in parts:
                    at = pl.multiple_of((place[2] ^ q) * piece, TAIL)
                    rows[2 * s + side, pl.ds(at, piece), :] = part[:piece, :]
                    top = jnp.maximum(top, part[piece:, :].astype(F32))
                scale_ref[s, side] = bound / top[:8, :]

    @pl.when(place[1] >= 0)
    def _():
        for k in range(2 * slots):
            lhs[k * LANES : (k + 1) * LANES, :] = rows[k].T

    for s in range(slots):
        out = jnp.dot(lhs[2 * s * LANES : 2 * (s + 1) * LANES, :], c_ref[...], preferred_element_type=F32)
        keep_ref[s] = out[:LANES] * scale_ref[s, 0, 0:1, 0:1]
        send_ref[s] = out[LANES:] * scale_ref[s, 1, 0:1, 0:1]


def product(place, own, gx, gy, dx, dy, matrix, vels):
    slots = own.shape[0]
    piece = own.shape[2] - TAIL
    depth, columns = matrix.shape
    out = jax.ShapeDtypeStruct((slots, LANES, columns), F32)
    vmem = pl.BlockSpec(memory_space=pltpu.VMEM)
    return pl.pallas_call(
        functools.partial(product_kernel, piece=piece, bound=HALF_MAX / (vels * columns * COLLISION_MAX)),
        out_shape=(out, out, jax.ShapeDtypeStruct((slots, 2, 8, LANES), F32)),
        in_specs=[pl.BlockSpec(memory_space=pltpu.SMEM)] + [vmem] * 6,
        out_specs=(vmem, vmem, vmem),
        scratch_shapes=[pltpu.VMEM((2 * slots, depth, LANES), BF16), pltpu.VMEM((slots * 2 * LANES, depth), BF16)],
        compiler_params=pltpu.CompilerParams(vmem_limit_bytes=8 << 20),
        cost_estimate=pl.CostEstimate(
            flops=2 * slots * 2 * LANES * depth * columns,
            bytes_accessed=depth * columns * 2 + slots * 2 * LANES * columns * 4,
            transcendentals=0,
        ),
        name="product",
    )(place, own, gx, gy, dx, dy, matrix)


def load_kernel(c_ref, out_ref, sem):
    copy = pltpu.make_async_copy(c_ref, out_ref, sem)
    copy.start()
    copy.wait()


def loaded(matrix):
    return pl.pallas_call(
        load_kernel,
        out_shape=jax.ShapeDtypeStruct(matrix.shape, matrix.dtype),
        in_specs=[pl.BlockSpec(memory_space=pltpu.HBM)],
        out_specs=pl.BlockSpec(memory_space=pltpu.VMEM),
        scratch_shapes=[pltpu.SemaphoreType.DMA],
        compiler_params=pltpu.CompilerParams(vmem_limit_bytes=1 << 20),
        cost_estimate=pl.CostEstimate(flops=1, bytes_accessed=2 * matrix.size * 2, transcendentals=0),
        name="load",
    )(matrix)


def edge_kernel(place, a_ref, c_ref, d_ref, out_ref, *, cells):
    chip, core = place[0], place[1]
    cell = 2 * chip + core
    last = cells // 2 - 1
    is_end = jnp.logical_or(chip == 0, chip == last)
    held = ((a_ref, jnp.where(is_end, 3, 0)), (c_ref, jnp.where(is_end, 1, 3)), (d_ref, jnp.where(is_end, 0, 1)))
    for k, other in enumerate(((cell + cells - 1) % cells, (cell + 1) % cells)):
        total = jnp.zeros((TAIL, LANES), F32)
        for ref, q in held:
            for side in range(2):
                here = jnp.logical_and((other // 2) ^ chip == q, (other % 2) ^ core == side)
                tail = ref[0, side, ref.shape[2] - TAIL :, :].astype(F32)
                total = total + jnp.where(here, tail, jnp.zeros_like(tail))
        out_ref[k] = total[:8] * (1.0 / HALF_MAX)


def edge_scales(place, a, c, d, cells):
    vmem = pl.BlockSpec(memory_space=pltpu.VMEM)
    return pl.pallas_call(
        functools.partial(edge_kernel, cells=cells),
        out_shape=jax.ShapeDtypeStruct((2, 8, LANES), F32),
        in_specs=[pl.BlockSpec(memory_space=pltpu.SMEM), vmem, vmem, vmem],
        out_specs=vmem,
        compiler_params=pltpu.CompilerParams(vmem_limit_bytes=4 << 20),
        cost_estimate=pl.CostEstimate(flops=10000, bytes_accessed=10000, transcendentals=0),
        name="edges",
    )(place, a, c, d)


def after(value, *earlier):
    return lax.optimization_barrier((value,) + earlier)[0]


def chain_body(distribution, collision, directions, wall_mask):
    tile_len, width, local_vel = distribution.shape
    cells = lax.axis_size("cell")
    cell = lax.axis_index("cell")
    vel = lax.axis_index("vel")
    place = jnp.stack([cell >> 1, cell & 1, vel])
    is_end = jnp.logical_or(cell < 2, cell >= cells - 2)
    distribution, place, is_end, offset = lax.optimization_barrier((distribution, place, is_end, vel * local_vel))
    matrix = collision.reshape(-1, local_vel)

    other_core = [(i, i ^ 1) for i in range(cells)]
    across = lambda q: [(i, 2 * ((i // 2) ^ q) + i % 2) for i in range(cells)]
    in_x = [(i, i ^ 1) for i in range(4)]
    in_y = [(i, i ^ 2) for i in range(4)]
    chips = lambda *pairs: [(2 * a + c, 2 * b + c) for a, b in pairs for c in range(2)]
    ends = chips((0, 1), (3, 2))
    middle = chips((1, 2), (2, 1))
    outward = chips((2, 3), (1, 0))
    ring = [(i, (i + 1) % cells) for i in range(cells)]

    def gather_x_y(own):
        return own, lax.ppermute(own, "vel", in_x), lax.ppermute(own, "vel", in_y)

    def gather_diagonal(parts, *earlier):
        own, gx, gy = parts
        dx = lax.ppermute(after(gx[:, 0], *earlier), "vel", in_y)
        dy = lax.ppermute(after(gy[:, 1], *earlier), "vel", in_x)
        return own, gx, gy, dx, dy

    def exchanged(mine, theirs):
        theirs = lax.ppermute(theirs.astype(F16), "cell", other_core)
        return [mine[s] + theirs[s].astype(F32) for s in range(mine.shape[0])]

    def behind(parts, *earlier):
        return (after(parts[0], *earlier),) + tuple(parts[1:])

    keep, send = split_pieces(distribution, place, cells)
    got = lax.ppermute(send, "cell", other_core)
    matrix = loaded(pltpu.with_memory_space_constraint(after(matrix, got), pltpu.HBM))
    both = [jnp.stack([keep[q], got[q]])[None] for q in range(4)]

    z3 = lax.ppermute(both[3], "cell", across(3))
    both1, both2, z3, matrix = lax.optimization_barrier((both[1], both[2], z3, matrix))
    ga = gather_x_y(jnp.where(is_end, z3, both[0]))
    slot_a = ga[0]
    slot_b = lax.ppermute(both2, "cell", across(2))
    z1 = lax.ppermute(both1, "cell", across(1))
    ga = gather_diagonal(ga)
    mine_a, theirs_a, scale_a = product(place, *ga, matrix, 4)
    theirs_a, slot_b, z1 = lax.optimization_barrier((theirs_a, slot_b, z1))
    (pa,) = exchanged(mine_a, theirs_a)
    ma = pa.astype(F16)
    a0 = lax.ppermute(ma, "cell", ends)
    gb = gather_x_y(after(slot_b, ma))
    gb = gather_diagonal(gb, ma)
    mine_b, theirs_b, _ = product(place, *gb, matrix, 4)
    (pb,) = exchanged(mine_b, theirs_b)
    mb = pb.astype(F16)
    mb1 = (pb + a0.astype(F32)).astype(F16)
    b1 = lax.ppermute(mb1, "cell", middle)
    a1 = lax.ppermute(after(mb, a0, mb1), "cell", ends)
    own_top = keep[0:1, keep.shape[1] - 1 :, 0:1].astype(F32)
    edges = after(distribution, a0) * (HALF_MAX / own_top)
    from_below = lax.ppermute(edges[tile_len - 2 :].astype(F16), "cell", ring)
    from_above = lax.ppermute(edges[:2].astype(F16), "cell", [(j, i) for i, j in ring])
    z1, z3, both0, _ = lax.optimization_barrier((z1, z3, both[0], gb[1]))
    slot_c = jnp.where(is_end, z1, z3)
    slot_d = jnp.where(is_end, both0, z1)
    gcd = gather_x_y(jnp.concatenate([slot_c, slot_d]))
    gcd = gather_diagonal(gcd, mb)
    mine_cd, theirs_cd, scale_cd = product(place, *behind(gcd, mb), matrix, 4)
    theirs_cd, from_below, from_above = lax.optimization_barrier((theirs_cd, from_below, from_above))
    pc, pd = exchanged(mine_cd, theirs_cd)
    mc2 = (pd + b1.astype(F32)).astype(F16)
    c2 = lax.ppermute(mc2, "cell", outward)
    a2 = lax.ppermute(after(pc.astype(F16), a1, mc2), "cell", ends)
    b2 = lax.ppermute((pc + a1.astype(F32)).astype(F16), "cell", middle)

    edge = edge_scales(place, *lax.optimization_barrier((slot_a, slot_c, slot_d, mb))[:3], cells)
    below = from_below.astype(F32) * edge[0:1, :1, :1]
    above = from_above.astype(F32) * edge[1:2, :1, :1]
    open_cells, base = advected(after(distribution, mb), below, above, directions, wall_mask, offset)
    scale = jnp.where(is_end, scale_cd[1, 0:1, :1, :1], scale_a[0, 0:1, :1, :1])
    own = jnp.where(is_end, pd, pa)
    factor = open_cells * (relax / scale)
    base, factor, own = lax.optimization_barrier((base, factor, own))
    arrived = a2.astype(F32) + b2.astype(F32) + c2.astype(F32)
    return base + factor * (own + arrived).reshape(distribution.shape)


def plain_body(distribution, collision, directions, wall_mask):
    tile_len, width, local_vel = distribution.shape
    cells = lax.axis_size("cell")
    vels = lax.axis_size("vel")
    cell = lax.axis_index("cell")
    piece = local_vel // cells
    up, down, around = halo_pairs(cells)
    head, foot = distribution[:2], distribution[tile_len - 2 :]
    from_around = lax.ppermute(jnp.where(cell == 0, head, foot), "cell", around)
    below = jnp.where(cell == 0, from_around, lax.ppermute(foot, "cell", up))
    above = jnp.where(cell == cells - 1, from_around, lax.ppermute(head, "cell", down))
    offset = lax.axis_index("vel") * local_vel
    open_cells, base = advected(distribution, below, above, directions, wall_mask, offset)
    pieces = distribution.astype(BF16).reshape(tile_len * width, cells, piece)
    spread = lax.all_to_all(pieces, "cell", split_axis=1, concat_axis=0, tiled=True)
    panel = lax.all_gather(spread.reshape(-1, piece), "vel", axis=1, tiled=True)
    part = jnp.dot(panel, collision.reshape(vels * piece, local_vel), preferred_element_type=F32)
    gain = lax.psum_scatter(part, "cell", scatter_dimension=0, tiled=True)
    return base + open_cells * relax * gain.reshape(distribution.shape)


def body(distribution, collision, directions, wall_mask):
    tile_len, width, local_vel = distribution.shape
    cells = lax.axis_size("cell")
    piece = local_vel // cells
    fits = tile_len * width == LANES and piece % TAIL == 0 and local_vel % (3 * LANES) == 0
    if cells == 8 and lax.axis_size("vel") == 4 and fits:
        return chain_body(distribution, collision, directions, wall_mask)
    return plain_body(distribution, collision, directions, wall_mask)


def solution(mesh):
    in_specs = (P("cell", None, "vel"), P(None, "cell", None, "vel"), P("vel"), P("cell", None))
    out_specs = P("cell", None, "vel")
    return jax.shard_map(body, mesh=mesh, in_specs=in_specs, out_specs=out_specs, check_vma=False)
```
